256 devices in a mesh: shot: 8 (over y, core), gx: 8 (over z), gy: 4 (over x).
Axes of the slice: x: 4, y: 4, z: 8, core: 2. Of those that a mesh axis runs over, the one named last changes fastest.
Arguments:
- vel_coef: float32 [256, 128, 128], P('gx', 'gy'), may hold values from 0.03 to 0.2
- src_prev: float32 [8, 256, 128, 128], P('shot', 'gx', 'gy'), may hold values from -6 to 6
- src_cur: float32 [8, 256, 128, 128], P('shot', 'gx', 'gy'), may hold values from -6 to 6
- rcv_prev: float32 [8, 256, 128, 128], P('shot', 'gx', 'gy'), may hold values from -6 to 6
- rcv_cur: float32 [8, 256, 128, 128], P('shot', 'gx', 'gy'), may hold values from -6 to 6
- src_pos: int32 [8], P('shot'), may hold values from 0 to 4194303
- src_amp: float32 [8, 3], P('shot'), may hold values from -24 to 24
- rcv_pos: int32 [8, 512], P('shot'), may hold values from 0 to 4194303
- rcv_data: float32 [8, 3, 512], P('shot'), may hold values from -6 to 6
- aperture: int32 [8, 16], P('shot'), may hold values from 0 to 31, as said below
- owner: int32 [32, 32], replicated, may hold values from 0 to 31, as said below
Outputs:
- src_next: float32 [8, 256, 128, 128], P('shot', 'gx', 'gy')
- rcv_next: float32 [8, 256, 128, 128], P('shot', 'gx', 'gy')
- gathers: float32 [32, 16, 32, 1, 32, 128], P(('gx', 'gy'), 'shot')
The draws below stay inside these ranges and needn't reach their ends.
Inputs may be any that keep to these rules, and one draw needn't show every extreme that they name: `aperture`: each row lists 16 different tiles. `owner`: each row and each column holds every tile number once.
All inputs are finite; a program needn't handle non-finite values.
Results may differ from the reference program's by a relative error of at most 0.0003.
Values sent between devices are 32-bit elements; how exact they have to be, the bound alone decides.
A program may use at most 64 MiB of HBM per device.

```python
import math
import jax
import jax.numpy as jnp
from jax import lax

CX = 32
CY = 32
OFFS = 16
STEPS = 3
RCV = 512
HALF = 8
SHOTS = 8
NT = 32
NAP = 16
SX = 1
NX = 256
NY = 128
NZ = 128
N_GX = 8
N_GY = 4


def draw_aperture(key, part):
    shot_keys = jax.random.split(jax.random.fold_in(key, 11), SHOTS)

    def choose_tiles(one_key):
        return jax.random.permutation(one_key, NT)[:NAP]
    return jax.vmap(choose_tiles)(shot_keys).astype(jnp.int32)


def draw_owner(key, part):
    relabel = jax.random.permutation(jax.random.fold_in(key, 21), NT)
    second = jax.random.permutation(jax.random.fold_in(key, 22), NT)
    row_index = jnp.arange(NT)[:, None]
    return relabel[(second[None, :] + row_index) % NT].astype(jnp.int32)


def plant(result, key, smallest, top_value):
    longest = result.shape.index(max(result.shape))
    spots = []
    for shift in (0, 1):
        where = [jax.random.randint(jax.random.fold_in(key, axis), (), 0, length) for axis, length in enumerate(result.shape)]
        where[longest] = (where[longest] + shift) % result.shape[longest]
        spots.append(tuple(where))
    return result.at[spots[0]].set(smallest).at[spots[1]].set(top_value)


def shard_levels(key, extent, pieces, smallest, largest):
    def one(position, blocks):
        steps = jax.random.uniform(jax.random.fold_in(jax.random.fold_in(key, 6), position), (blocks,), jnp.float32, smallest / len(pieces), largest / len(pieces))
        return jnp.repeat(jnp.exp(steps), extent[position] // blocks).reshape((-1,) + (1,) * (len(extent) - position - 1))

    level = one(*pieces[0])
    for cut in pieces[1:]:
        level = level * one(*cut)
    return level


def centred(own_key, shape, width, reach, shards=(), kind=jnp.bfloat16):
    factor_of = shard_levels(own_key, shape, shards, -0.22, 0.18) if shards else 1.0
    array = jax.random.normal(own_key, shape, jnp.float32) * width * factor_of
    return jnp.minimum(jnp.maximum(array, -reach), reach).astype(kind)


def setup_inputs(seed: int = 0) -> dict:
    keys = jax.random.split(jax.random.key(seed), 12)
    return {
        "vel_coef": jnp.clip(jnp.exp(math.log(0.2) - 1.89712 * jax.random.uniform(keys[0], (NX, NY, NZ), jnp.float32) ** shard_levels(keys[0], (NX, NY, NZ), ((0, 8), (1, 4)), -0.2, 0.2)), 0.03, 0.2),
        "src_prev": centred(keys[1], (SHOTS, NX, NY, NZ), 1.0, 6.0, ((0, 8), (1, 8), (2, 4)), jnp.float32),
        "src_cur": centred(keys[2], (SHOTS, NX, NY, NZ), 1.0, 6.0, ((0, 8), (1, 8), (2, 4)), jnp.float32),
        "rcv_prev": centred(keys[3], (SHOTS, NX, NY, NZ), 1.0, 6.0, ((0, 8), (1, 8), (2, 4)), jnp.float32),
        "rcv_cur": centred(keys[4], (SHOTS, NX, NY, NZ), 1.0, 6.0, ((0, 8), (1, 8), (2, 4)), jnp.float32),
        "src_pos": plant(jax.random.randint(keys[5], (SHOTS,), 0, NX * NY * NZ), jax.random.fold_in(keys[5], 1), 0, (NX * NY * NZ) - 1).astype(jnp.int32),
        "src_amp": centred(keys[6], (SHOTS, STEPS), 4.0, 24.0, ((0, 8),), jnp.float32),
        "rcv_pos": plant(jax.random.randint(keys[7], (SHOTS, RCV), 0, NX * NY * NZ), jax.random.fold_in(keys[7], 1), 0, (NX * NY * NZ) - 1).astype(jnp.int32),
        "rcv_data": centred(keys[8], (SHOTS, STEPS, RCV), 2.0, 6.0, ((0, 8),), jnp.float32),
        "aperture": draw_aperture(jax.random.fold_in(keys[11], 71), 0),
        "owner": draw_owner(jax.random.fold_in(keys[11], 71), 0),
    }


LAP_CENTER = -2.5
LAP_NEAR = 4.0 / 3.0
LAP_FAR = -1.0 / 12.0


def laplacian(widened):
    centre = widened[..., 2:-2, 2:-2, :]
    summed = 3.0 * LAP_CENTER * centre
    summed = summed + LAP_NEAR * (widened[..., 3:-1, 2:-2, :] + widened[..., 1:-3, 2:-2, :])
    summed = summed + LAP_FAR * (widened[..., 4:, 2:-2, :] + widened[..., :-4, 2:-2, :])
    summed = summed + LAP_NEAR * (widened[..., 2:-2, 3:-1, :] + widened[..., 2:-2, 1:-3, :])
    summed = summed + LAP_FAR * (widened[..., 2:-2, 4:, :] + widened[..., 2:-2, :-4, :])
    depth_pad = jnp.pad(centre, [(0, 0)] * (centre.ndim - 1) + [(2, 2)])
    summed = summed + LAP_NEAR * (depth_pad[..., 3:-1] + depth_pad[..., 1:-3])
    summed = summed + LAP_FAR * (depth_pad[..., 4:] + depth_pad[..., :-4])
    return summed


def inject_flat(field_in, positions, values):
    flat_field = field_in.reshape(-1).at[positions].add(values)
    return flat_field.reshape(field_in.shape)


def advance(previous, current, vel_coef):
    padded = jnp.pad(current, ((2, 2), (2, 2), (0, 0)))
    return 2.0 * current - previous + vel_coef * laplacian(padded)


def reference(vel_coef, src_prev, src_cur, rcv_prev, rcv_cur, src_pos, src_amp, rcv_pos, rcv_data, aperture, owner):
    tile_numbers = ((jnp.arange(NX) // CX)[:, None] * N_GY + (jnp.arange(NY) // CY)[None, :]).astype(jnp.int32)

    def one_shot(image, shot_items):
        src_old, src_now, rcv_old, rcv_now, src_where, src_wave, rcv_where, rcv_wave, ap_row = shot_items
        cell_mask = jnp.any(tile_numbers[:, :, None] == ap_row[None, None, :], axis=2).astype(jnp.float32)
        snapshots = []
        for step_index in range(STEPS):
            src_new = inject_flat(advance(src_old, src_now, vel_coef), src_where, src_wave[step_index])
            rcv_new = inject_flat(advance(rcv_old, rcv_now, vel_coef), rcv_where, rcv_wave[step_index])
            src_old, src_now = src_now, src_new
            rcv_old, rcv_now = rcv_now, rcv_new
            snapshots.append((jnp.pad(src_now, ((HALF, HALF), (0, 0), (0, 0))), jnp.pad(rcv_now, ((HALF, HALF), (0, 0), (0, 0)))))
        offset_rows = []
        for offset_index in range(OFFS):
            lead_start = 2 * HALF - offset_index
            summed = None
            for src_ext, rcv_ext in snapshots:
                product_term = src_ext[lead_start:lead_start + NX] * rcv_ext[offset_index:offset_index + NX]
                summed = product_term if summed is None else summed + product_term
            offset_rows.append(summed)
        contribution = jnp.stack(offset_rows) * cell_mask[None, :, :, None]
        return image + contribution, (src_now, rcv_now)

    image_start = jnp.zeros((OFFS, NX, NY, NZ), jnp.float32)
    image, (src_next, rcv_next) = lax.scan(one_shot, image_start, (src_prev, src_cur, rcv_prev, rcv_cur, src_pos, src_amp, rcv_pos, rcv_data, aperture))
    strips = image.reshape(OFFS, N_GX, NT, SX, N_GY, CY, NZ)
    strips = jnp.transpose(strips, (1, 4, 2, 0, 3, 5, 6)).reshape(NT, NT, OFFS, SX, CY, NZ)
    matches = owner[:, :, None] == jnp.arange(NT, dtype=jnp.int32)[None, None, :]
    strip_for = jnp.sum(jnp.where(matches, jnp.arange(NT, dtype=jnp.int32)[None, :, None], 0), axis=1).astype(jnp.int32)
    picked = jax.vmap(lambda tile_strips, tile_index: jnp.take(tile_strips, tile_index, axis=0))(strips, strip_for)
    gathers = jnp.transpose(picked, (1, 2, 0, 3, 4, 5))
    return src_next, rcv_next, gathers
```

```python
import jax
import jax.numpy as jnp
from jax import lax
from jax.experimental import pallas as pl
from jax.experimental.pallas import tpu as pltpu
from jax.sharding import PartitionSpec as P

MESH = pl.DeviceIdType.MESH
OFFS = 16
STEPS = 3
HALF = 8
NEAR = 4.0 / 3.0
FAR = -1.0 / 12.0
CENTRE = 3.0 * -2.5

CX, CY, NZ = 32, 32, 128
N_GX, N_GY, N_SHOT = 8, 4, 8
TILES = N_GX * N_GY
GROUPS = 4
SG = TILES // GROUPS
CHIPS = N_SHOT // 2
EXT = CX + 2 * HALF
F32 = jnp.float32


def prepare_kernel(pos_ref, data_ref, spos_ref, ap_ref, owner_ref, inj_ref, strip_ref, mask_ref, src_ref):
    gx, gy = lax.axis_index("gx"), lax.axis_index("gy")
    tile = gx * N_GY + gy

    def invert(k, carry):
        strip_ref[owner_ref[tile, k]] = k
        return carry

    lax.fori_loop(0, TILES, invert, 0)
    hit = jnp.int32(0)
    for i in range(ap_ref.shape[1]):
        hit = jnp.where(ap_ref[0, i] == tile, jnp.int32(1), hit)
    mask_ref[0] = hit.astype(F32)
    p = spos_ref[0]
    lx = lax.shift_right_logical(p, 14) - gx * CX
    ly = (lax.shift_right_logical(p, 7) & 127) - gy * CY
    inside = (lx >= 0) & (lx < CX) & (ly >= 0) & (ly < CY)
    src_ref[0] = jnp.where(inside, (lx * CY + ly) * NZ + (p & 127), -1)

    pos = pos_ref[...]
    rx = lax.shift_right_logical(pos, 14) - gx * CX
    ry = (lax.shift_right_logical(pos, 7) & 127) - gy * CY
    rz = pos & 127
    ok = (rx >= 0) & (rx < CX) & (ry >= 0) & (ry < CY)
    cell = jnp.where(ok, rx * CY + ry, -1)
    n = pos.shape[1]
    depth = lax.broadcasted_iota(jnp.int32, (NZ, n), 0) == rz
    parts = [[], [], []]
    for t in range(STEPS):
        left = jnp.where(depth, data_ref[0, t : t + 1, :], 0.0)
        for piece in parts:
            cut = left.astype(jnp.bfloat16)
            piece.append(cut)
            left = left - cut.astype(F32)
    parts = [jnp.concatenate(piece, axis=0) for piece in parts]
    rows = 256
    for first in range(0, CX * CY, rows):
        spot = lax.broadcasted_iota(jnp.int32, (rows, n), 0) + first == cell
        spot = jnp.where(spot, 1.0, 0.0).astype(jnp.bfloat16)
        total = None
        for piece in parts:
            term = lax.dot_general(spot, piece, (((1,), (1,)), ((), ())), preferred_element_type=F32)
            total = term if total is None else total + term
        for t in range(STEPS):
            inj_ref[t, first : first + rows, :] = total[:, t * NZ : (t + 1) * NZ]


def prepare(rcv_pos, rcv_data, src_pos, aperture, owner):
    smem = pl.BlockSpec(memory_space=pltpu.SMEM)
    vmem = pl.BlockSpec(memory_space=pltpu.VMEM)
    return pl.pallas_call(
        prepare_kernel,
        out_shape=(
            jax.ShapeDtypeStruct((STEPS, CX * CY, NZ), F32),
            jax.ShapeDtypeStruct((TILES,), jnp.int32),
            jax.ShapeDtypeStruct((1,), F32),
            jax.ShapeDtypeStruct((1,), jnp.int32),
        ),
        in_specs=[vmem, vmem, smem, smem, smem],
        out_specs=(vmem, smem, smem, smem),
        name="prepare",
    )(rcv_pos, rcv_data, src_pos, aperture, owner)


def main_kernel(
    vel, s_prev, s_cur, r_prev, r_cur, inj, strip, mask, src, amp,
    s_out, r_out, g_out,
    w0, w1, w2, w3, old, speed, drive, ysend, yrecv, part, mate, ring1, ring2, final,
    load_sem, xs_sem, xr_sem, ys_sem, yr_sem, a_sem, b_sem, c_sem, e_sem, out_sem,
):
    gx, gy, shot = lax.axis_index("gx"), lax.axis_index("gy"), lax.axis_index("shot")
    core = lax.rem(shot, 2)
    chip = lax.div(shot, 2)
    tile = gx * N_GY + gy
    fields = (w0, w1, w2, w3)
    has_left, has_right = gx > 0, gx < N_GX - 1
    has_low, has_high = gy > 0, gy < N_GY - 1
    other = {"shot": shot + 1 - 2 * core}
    above = {"shot": lax.rem(shot + 2, N_SHOT)}
    below = {"shot": lax.rem(shot + N_SHOT - 2, N_SHOT)}

    barrier = pltpu.get_barrier_semaphore()
    for peer in (other, above, below):
        pl.semaphore_signal(barrier, inc=1, device_id=peer, device_id_type=MESH)

    def greet(j, carry):
        peer = lax.rem(tile + j, TILES)
        pl.semaphore_signal(
            barrier, inc=1, device_id={"gx": lax.div(peer, N_GY), "gy": lax.rem(peer, N_GY)},
            device_id_type=MESH,
        )
        return carry

    lax.fori_loop(1, TILES, greet, 0)

    inner = (slice(HALF, HALF + CX), slice(HALF, HALF + CY))
    loads = [
        pltpu.make_async_copy(s_cur.at[0], w0.at[(0,) + inner], load_sem.at[0]),
        pltpu.make_async_copy(r_cur.at[0], w0.at[(1,) + inner], load_sem.at[1]),
        pltpu.make_async_copy(s_prev.at[0], old.at[0], load_sem.at[2]),
        pltpu.make_async_copy(r_prev.at[0], old.at[1], load_sem.at[3]),
        pltpu.make_async_copy(vel, speed, load_sem.at[4]),
        pltpu.make_async_copy(inj, drive, load_sem.at[5]),
    ]
    for copy in loads:
        copy.start()

    def clear_x(first, count):
        for w in fields:
            lo, n = (first, count) if w is not w0 else ((6, 2) if first == 0 else (40, 2))

            def body(i, carry, w=w, lo=lo):
                w[0, lo + i, HALF : HALF + CY, :] = jnp.zeros((CY, NZ), F32)
                w[1, lo + i, HALF : HALF + CY, :] = jnp.zeros((CY, NZ), F32)
                return carry

            lax.fori_loop(0, n, body, 0)

    def clear_y(first):
        for w in fields[:STEPS]:

            def body(i, carry, w=w):
                w[0, HALF + i, first : first + 8, :] = jnp.zeros((8, NZ), F32)
                w[1, HALF + i, first : first + 8, :] = jnp.zeros((8, NZ), F32)
                return carry

            lax.fori_loop(0, CX, body, 0)

    pl.when(jnp.logical_not(has_left))(lambda: clear_x(0, HALF))
    pl.when(jnp.logical_not(has_right))(lambda: clear_x(HALF + CX, HALF))
    pl.when(jnp.logical_not(has_low))(lambda: clear_y(0))
    pl.when(jnp.logical_not(has_high))(lambda: clear_y(HALF + CY))

    def x_copy(t, way, piece):
        w = fields[t]
        if way == 0:
            here, there = ((38, 6), (32, 0))[piece]
            to = {"gx": gx + 1}
        else:
            here, there = ((8, 40), (10, 42))[piece]
            to = {"gx": gx - 1}
        n = (2, 6)[piece]
        return pltpu.make_async_remote_copy(
            src_ref=w.at[:, here : here + n, HALF : HALF + CY, :],
            dst_ref=w.at[:, there : there + n, HALF : HALF + CY, :],
            send_sem=xs_sem.at[t, way, piece],
            recv_sem=xr_sem.at[t, way, piece],
            device_id=to,
            device_id_type=MESH,
        )

    def y_copy(t, way):
        return pltpu.make_async_remote_copy(
            src_ref=ysend.at[t, way],
            dst_ref=yrecv.at[t, way],
            send_sem=ys_sem.at[t, way],
            recv_sem=yr_sem.at[t, way],
            device_id={"gy": gy + 1 - 2 * way},
            device_id_type=MESH,
        )

    x_to = (has_right, has_left)
    x_from = (has_left, has_right)
    y_to = (has_high, has_low)
    y_from = (has_low, has_high)

    def send_x(t, piece):
        for way in range(2):
            pl.when(x_to[way])(lambda: x_copy(t, way, piece).start())

    def got_x(t, piece):
        for way in range(2):
            pl.when(x_from[way])(lambda: x_copy(t, way, piece).wait_recv())

    def pack_y(t):
        w = fields[t]

        def body(i, carry):
            for f in range(2):
                for j in range(4):
                    row = pl.ds(f * 2 * CX + pl.multiple_of(i * 8, 8) + 2 * j, 2)
                    ysend[t, 0, row, :] = w[f, HALF + i * 4 + j, HALF + CY - 2 : HALF + CY, :]
                    ysend[t, 1, row, :] = w[f, HALF + i * 4 + j, HALF : HALF + 2, :]
            return carry

        lax.fori_loop(0, CX // 4, body, 0)

    def unpack_y(t, way):
        w = fields[t]
        at = HALF - 2 if way == 0 else HALF + CY

        def body(i, carry):
            for f in range(2):
                for j in range(4):
                    row = pl.ds(f * 2 * CX + pl.multiple_of(i * 8, 8) + 2 * j, 2)
                    w[f, HALF + i * 4 + j, at : at + 2, :] = yrecv[t, way, row, :]
            return carry

        lax.fori_loop(0, CX // 4, body, 0)

    def send_y(t):
        pack_y(t)
        for way in range(2):
            pl.when(y_to[way])(lambda: y_copy(t, way).start())

    def got_y(t):
        for way in range(2):

            def body(way=way):
                y_copy(t, way).wait_recv()
                unpack_y(t, way)

            pl.when(y_from[way])(body)

    lane = lax.broadcasted_iota(jnp.int32, (8, NZ), 1)
    near_up = jnp.where(lane < NZ - 1, NEAR, 0.0)
    near_down = jnp.where(lane > 0, NEAR, 0.0)
    far_up = jnp.where(lane < NZ - 2, FAR, 0.0)
    far_down = jnp.where(lane > 1, FAR, 0.0)
    spot = lax.broadcasted_iota(jnp.int32, (8, NZ), 0) * NZ + lane

    def advance(t):
        w, new = fields[t], fields[t + 1]
        where = src[0]
        push = amp[0, t]

        def body(x, carry):
            X = x + HALF
            for y in range(CY // 8):
                Y = HALF + 8 * y
                v = speed[x, 8 * y : 8 * y + 8, :]
                for f in range(2):
                    c = w[f, X, Y : Y + 8, :]
                    lap = CENTRE * c
                    lap = lap + NEAR * (w[f, X + 1, Y : Y + 8, :] + w[f, X - 1, Y : Y + 8, :])
                    lap = lap + FAR * (w[f, X + 2, Y : Y + 8, :] + w[f, X - 2, Y : Y + 8, :])
                    lap = lap + NEAR * (w[f, X, Y + 1 : Y + 9, :] + w[f, X, Y - 1 : Y + 7, :])
                    lap = lap + FAR * (w[f, X, Y + 2 : Y + 10, :] + w[f, X, Y - 2 : Y + 6, :])
                    lap = lap + near_up * pltpu.roll(c, NZ - 1, 1) + near_down * pltpu.roll(c, 1, 1)
                    lap = lap + far_up * pltpu.roll(c, NZ - 2, 1) + far_down * pltpu.roll(c, 2, 1)
                    if t == 0:
                        before = old[f, x, 8 * y : 8 * y + 8, :]
                    else:
                        before = fields[t - 1][f, X, Y : Y + 8, :]
                    value = 2.0 * c - before + v * lap
                    if f == 0:
                        add = jnp.where(spot == where - (x * CY + 8 * y) * NZ, push, 0.0)
                    else:
                        add = drive[t, pl.ds(pl.multiple_of(x * CY + 8 * y, 8), 8), :]
                    new[f, X, Y : Y + 8, :] = value + add
            return carry

        lax.fori_loop(0, CX, body, 0)

    for copy in loads[:2]:
        copy.wait()
    pl.semaphore_wait(barrier, TILES - 1 + 3)
    send_x(0, 0)
    send_y(0)
    for copy in loads[2:]:
        copy.wait()
    for t in range(STEPS):
        got_x(t, 0)
        got_y(t)
        advance(t)
        send_x(t + 1, 0)
        if t + 1 < STEPS:
            send_y(t + 1)
        send_x(t + 1, 1)

    store_s = pltpu.make_async_copy(w3.at[(0,) + inner], s_out.at[0], out_sem.at[0])
    store_r = pltpu.make_async_copy(w3.at[(1,) + inner], r_out.at[0], out_sem.at[1])
    store_s.start()
    store_r.start()

    got_x(STEPS, 0)
    for t in range(1, STEPS + 1):
        got_x(t, 1)

    m = mask[0]
    dxs = (2, 1, 3, 0)
    dzs = (4, 3, 5, 2, 6, 1, 7, 0)

    def to_whom(group, i):
        dx = jnp.int32(dxs[0])
        for g in range(1, GROUPS):
            dx = jnp.where(group == g, dxs[g], dx)
        dz = jnp.int32(dzs[0])
        for j in range(1, SG):
            dz = jnp.where(i == j, dzs[j], dz)
        return lax.rem(gx + dz, N_GX), lax.rem(gy + dx, N_GY)

    def correlate(group):
        def body(i, carry):
            ox, oy = to_whom(group, i)
            k = strip[ox * N_GY + oy]
            for y in range(CY // 8):
                Y = HALF + 8 * y
                for h in range(OFFS):
                    total = None
                    for w in (w1, w2, w3):
                        term = w[0, k + OFFS - h, Y : Y + 8, :] * w[1, k + h, Y : Y + 8, :]
                        total = term if total is None else total + term
                    away = lax.rem((h // 2) % 2 + core, 2)
                    part[away, group, h // 4, h % 2, i, 8 * y : 8 * y + 8, :] = total * m
            return carry

        lax.fori_loop(0, SG, body, 0)

    def a_copy(group):
        return pltpu.make_async_remote_copy(
            src_ref=part.at[1, group], dst_ref=mate.at[group],
            send_sem=a_sem.at[0, group], recv_sem=a_sem.at[1, group],
            device_id=other, device_id_type=MESH,
        )

    def b_copy(group, way):
        return pltpu.make_async_remote_copy(
            src_ref=part.at[0, group, lax.rem(chip + 2, CHIPS), way], dst_ref=ring1.at[group, way],
            send_sem=b_sem.at[0, group, way], recv_sem=b_sem.at[1, group, way],
            device_id=(above, below)[way], device_id_type=MESH,
        )

    def c_copy(group, way):
        return pltpu.make_async_remote_copy(
            src_ref=part.at[0, group, lax.rem(chip + (1, 3)[way], CHIPS)], dst_ref=ring2.at[group, way],
            send_sem=c_sem.at[0, group, way], recv_sem=c_sem.at[1, group, way],
            device_id=(above, below)[way], device_id_type=MESH,
        )

    def e_copy(group, i):
        ox, oy = to_whom(group, i)
        return pltpu.make_async_remote_copy(
            src_ref=final.at[group * SG + i], dst_ref=g_out.at[0, :, tile, 0],
            send_sem=e_sem.at[0], recv_sem=e_sem.at[1],
            device_id={"gx": ox, "gy": oy}, device_id_type=MESH,
        )

    def own_copy():
        return pltpu.make_async_copy(final.at[TILES - 1], g_out.at[0, :, tile, 0], e_sem.at[2])

    def add_mate(group, which):
        def body(i, carry):
            for h in range(2):
                part[0, group, which, h, i] = part[0, group, which, h, i] + mate[group, which, h, i]
            return carry

        lax.fori_loop(0, SG, body, 0)

    def from_mate(group):
        a_copy(group).wait_recv()
        add_mate(group, lax.rem(chip + 2, CHIPS))
        for way in range(2):
            b_copy(group, way).start()
        for far in (1, 3, 0):
            add_mate(group, lax.rem(chip + far, CHIPS))

    def from_ring1(group):
        for way in range(2):
            b_copy(group, way).wait_recv()
            which = lax.rem(chip + (1, 3)[way], CHIPS)

            def body(i, carry):
                part[0, group, which, way, i] = part[0, group, which, way, i] + ring1[group, way, i]
                return carry

            lax.fori_loop(0, SG, body, 0)
            c_copy(group, way).start()

    def from_ring2(group):
        for way in range(2):
            c_copy(group, way).wait_recv()

        def body(i, carry):
            for h in range(2):
                final[group * SG + i, h] = (
                    part[0, group, chip, h, i] + ring2[group, 0, h, i] + ring2[group, 1, h, i]
                )
            mine = (group == GROUPS - 1) & (i == SG - 1)

            @pl.when(mine)
            def _():
                own_copy().start()

            @pl.when(jnp.logical_not(mine))
            def _():
                e_copy(group, i).start()

            return carry

        lax.fori_loop(0, SG, body, 0)

    def stage(it, carry):
        @pl.when(it < GROUPS)
        def _():
            correlate(it)
            a_copy(it).start()

        @pl.when((it >= 1) & (it < GROUPS + 1))
        def _():
            from_mate(it - 1)

        @pl.when((it >= 2) & (it < GROUPS + 2))
        def _():
            from_ring1(it - 2)

        @pl.when(it >= 3)
        def _():
            from_ring2(it - 3)

        return carry

    lax.fori_loop(0, GROUPS + 3, stage, 0)

    for t in range(STEPS + 1):
        for way in range(2):
            for piece in range(2 if t else 1):
                pl.when(x_to[way])(lambda: x_copy(t, way, piece).wait_send())
    for t in range(STEPS):
        for way in range(2):
            pl.when(y_to[way])(lambda: y_copy(t, way).wait_send())

    def drain(group, carry):
        a_copy(group).wait_send()
        for way in range(2):
            b_copy(group, way).wait_send()
            c_copy(group, way).wait_send()
        return carry

    lax.fori_loop(0, GROUPS, drain, 0)
    store_s.wait()
    store_r.wait()
    own_copy().wait()
    pltpu.make_async_copy(final.at[0 : TILES - 1], final.at[0 : TILES - 1], e_sem.at[0]).wait()
    arrived = g_out.at[0, :, 0 : TILES - 1, 0]
    pltpu.make_async_copy(arrived, arrived, e_sem.at[1]).wait()


def body(vel_coef, src_prev, src_cur, rcv_prev, rcv_cur, src_pos, src_amp, rcv_pos, rcv_data, aperture, owner):
    inj, strip, mask, src = prepare(rcv_pos, rcv_data, src_pos, aperture, owner)
    whole = pl.BlockSpec(memory_space=pl.ANY)
    smem = pl.BlockSpec(memory_space=pltpu.SMEM)
    DMA = pltpu.SemaphoreType.DMA
    wave = pltpu.VMEM((2, EXT, CY + 16, NZ), F32)
    return pl.pallas_call(
        main_kernel,
        out_shape=(
            jax.ShapeDtypeStruct(src_cur.shape, F32),
            jax.ShapeDtypeStruct(rcv_cur.shape, F32),
            jax.ShapeDtypeStruct((1, 2, TILES, 1, CY, NZ), F32),
        ),
        in_specs=[whole] * 6 + [smem] * 4,
        out_specs=(whole, whole, whole),
        scratch_shapes=[
            wave, wave, wave, wave,
            pltpu.VMEM((2, CX, CY, NZ), F32),
            pltpu.VMEM((CX, CY, NZ), F32),
            pltpu.VMEM((STEPS, CX * CY, NZ), F32),
            pltpu.VMEM((STEPS, 2, 4 * CX, NZ), F32),
            pltpu.VMEM((STEPS, 2, 4 * CX, NZ), F32),
            pltpu.VMEM((2, GROUPS, CHIPS, 2, SG, CY, NZ), F32),
            pltpu.VMEM((GROUPS, CHIPS, 2, SG, CY, NZ), F32),
            pltpu.VMEM((GROUPS, 2, SG, CY, NZ), F32),
            pltpu.VMEM((GROUPS, 2, 2, SG, CY, NZ), F32),
            pltpu.VMEM((TILES, 2, CY, NZ), F32),
            DMA((6,)),
            DMA((STEPS + 1, 2, 2)),
            DMA((STEPS + 1, 2, 2)),
            DMA((STEPS, 2)),
            DMA((STEPS, 2)),
            DMA((2, GROUPS)),
            DMA((2, GROUPS, 2)),
            DMA((2, GROUPS, 2)),
            DMA((3,)),
            DMA((2,)),
        ],
        compiler_params=pltpu.CompilerParams(
            collective_id=0, has_side_effects=True, vmem_limit_bytes=48 * 1024 * 1024
        ),
        name="migrate",
    )(vel_coef, src_prev, src_cur, rcv_prev, rcv_cur, inj, strip, mask, src, src_amp)


def solution(mesh):
    return jax.shard_map(
        body,
        mesh=mesh,
        in_specs=(
            P("gx", "gy", None),
            P("shot", "gx", "gy", None),
            P("shot", "gx", "gy", None),
            P("shot", "gx", "gy", None),
            P("shot", "gx", "gy", None),
            P("shot"),
            P("shot", None),
            P("shot", None),
            P("shot", None, None),
            P("shot", None),
            P(),
        ),
        out_specs=(
            P("shot", "gx", "gy", None),
            P("shot", "gx", "gy", None),
            P(("gx", "gy"), "shot", None, None, None, None),
        ),
        check_vma=False,
    )
```

```python
import jax
import jax.numpy as jnp
from jax import lax
from jax.experimental import pallas as pl
from jax.experimental.pallas import tpu as pltpu
from jax.sharding import PartitionSpec as P

MESH = pl.DeviceIdType.MESH
OFFS = 16
STEPS = 3
HALF = 8
NEAR = 4.0 / 3.0
FAR = -1.0 / 12.0
CENTRE = 3.0 * -2.5

CX, CY, NZ = 32, 32, 128
N_GX, N_GY, N_SHOT = 8, 4, 8
TILES = N_GX * N_GY
GROUPS = 4
SG = TILES // GROUPS
CHIPS = N_SHOT // 2
EDGE = 2
EXT = CX + 2 * HALF
BAND = 8
F32 = jnp.float32


def main_kernel(
    vel, s_prev, s_cur, r_prev, r_cur, pos_ref, data_ref, ap_ref, owner_ref, spos, amp,
    s_out, r_out, g_out,
    w0, w1, w2, w3, bands, old, speed, drive, ysend, yrecv, part, half, final, masks, strip_v, strip,
    load_sem, xs_sem, xr_sem, ys_sem, yr_sem, ms_sem, mr_sem, es_sem, er_sem, zs_sem, zr_sem,
    bs_sem, br_sem, cs_sem, cr_sem, d_sem, out_sem,
):
    gx, gy, shot = lax.axis_index("gx"), lax.axis_index("gy"), lax.axis_index("shot")
    core = lax.rem(shot, 2)
    chip = lax.div(shot, 2)
    tile = gx * N_GY + gy
    fields = (w0, w1, w2, w3)
    has_left, has_right = gx > 0, gx < N_GX - 1
    has_low, has_high = gy > 0, gy < N_GY - 1

    def pair_a(c):
        return c + 1 - 2 * lax.rem(c, 2)

    def pair_b(c):
        return CHIPS - 1 - c

    def band_a(c):
        return lax.rem(lax.div(c + 1, 2), 2)

    def band_b(c):
        return 2 + lax.div(c, 2)

    chip_a, chip_b = pair_a(chip), pair_b(chip)
    first = jnp.where(core == 0, chip_a, chip_b)
    second = jnp.where(core == 0, chip_b, chip_a)
    band = jnp.where(core == 0, band_a(chip), band_b(chip))
    mate = {"shot": shot + 1 - 2 * core}
    peers = (mate, {"shot": 2 * chip_a}, {"shot": 2 * chip_a + 1}, {"shot": 2 * chip_b}, {"shot": 2 * chip_b + 1})

    barrier = pltpu.get_barrier_semaphore()
    for peer in peers:
        pl.semaphore_signal(barrier, inc=1, device_id=peer, device_id_type=MESH)

    def greet(j, carry):
        peer = lax.rem(tile + j, TILES)
        pl.semaphore_signal(
            barrier, inc=1, device_id={"gx": lax.div(peer, N_GY), "gy": lax.rem(peer, N_GY)},
            device_id_type=MESH,
        )
        return carry

    lax.fori_loop(1, TILES, greet, 0)

    inner = (slice(EDGE, EDGE + CX), slice(8, 8 + CY))
    loads = [
        pltpu.make_async_copy(s_cur.at[0], w0.at[(0,) + inner], load_sem.at[0]),
        pltpu.make_async_copy(r_cur.at[0], w0.at[(1,) + inner], load_sem.at[1]),
        pltpu.make_async_copy(s_prev.at[0], old.at[0], load_sem.at[2]),
        pltpu.make_async_copy(r_prev.at[0], old.at[1], load_sem.at[3]),
        pltpu.make_async_copy(vel, speed, load_sem.at[4]),
    ]
    for copy in loads:
        copy.start()

    row = owner_ref[pl.ds(tile, 1), :]
    match = row == lax.broadcasted_iota(jnp.int32, (TILES, TILES), 0)
    number = lax.broadcasted_iota(jnp.int32, (TILES, TILES), 1)
    found = jnp.max(jnp.where(match, number, 0), axis=1, keepdims=True)
    strip_v[...] = jnp.broadcast_to(found, (TILES, NZ))
    table = pltpu.make_async_copy(strip_v, strip, load_sem.at[5])
    table.start()
    hit = jnp.max(jnp.where(ap_ref[...] == tile, 1.0, 0.0), axis=1, keepdims=True)
    masks[0] = jnp.broadcast_to(hit, (8, NZ))

    def clear_x(at, wide):
        def body(i, carry):
            for w in fields[:STEPS]:
                for f in range(2):
                    w[f, at + i, 8 : 8 + CY, :] = jnp.zeros((CY, NZ), F32)
            return carry

        lax.fori_loop(0, EDGE, body, 0)

        def body2(i, carry):
            for t in range(STEPS):
                for s in range(4):
                    for f in range(2):
                        bands[t, s, f, wide + i] = jnp.zeros((BAND, NZ), F32)
            return carry

        lax.fori_loop(0, HALF, body2, 0)

    def clear_y(at):
        def body(i, carry):
            for w in fields[:STEPS]:
                for f in range(2):
                    w[f, EDGE + i, at : at + 8, :] = jnp.zeros((8, NZ), F32)
            return carry

        lax.fori_loop(0, CX, body, 0)

    pl.when(jnp.logical_not(has_left))(lambda: clear_x(0, 0))
    pl.when(jnp.logical_not(has_right))(lambda: clear_x(EDGE + CX, HALF + CX))
    pl.when(jnp.logical_not(has_low))(lambda: clear_y(0))
    pl.when(jnp.logical_not(has_high))(lambda: clear_y(8 + CY))

    def inject():
        pos = pos_ref[...]
        rx = lax.shift_right_logical(pos, 14) - gx * CX
        ry = (lax.shift_right_logical(pos, 7) & 127) - gy * CY
        ok = (rx >= 0) & (rx < CX) & (ry >= 0) & (ry < CY)
        cell = jnp.where(ok, rx * CY + ry, -1)
        n = pos.shape[1]
        depth = lax.broadcasted_iota(jnp.int32, (NZ, n), 0) == (pos & 127)
        parts = [[], [], []]
        for t in range(STEPS):
            left = jnp.where(depth, data_ref[t], 0.0)
            for piece in parts:
                cut = left.astype(jnp.bfloat16)
                piece.append(cut)
                left = left - cut.astype(F32)
        parts = [jnp.concatenate(piece, axis=0) for piece in parts]
        rows = 256
        for at in range(0, CX * CY, rows):
            spot = lax.broadcasted_iota(jnp.int32, (rows, n), 0) + at == cell
            spot = jnp.where(spot, 1.0, 0.0).astype(jnp.bfloat16)
            total = None
            for piece in parts:
                term = lax.dot_general(spot, piece, (((1,), (1,)), ((), ())), preferred_element_type=F32)
                total = term if total is None else total + term
            for t in range(STEPS):
                drive[t, at : at + rows, :] = total[:, t * NZ : (t + 1) * NZ]

    inject()

    def x_copy(t, way):
        here, there = ((CX, 0), (EDGE, EDGE + CX))[way]
        return pltpu.make_async_remote_copy(
            src_ref=fields[t].at[:, here : here + EDGE, 8 : 8 + CY, :],
            dst_ref=fields[t].at[:, there : there + EDGE, 8 : 8 + CY, :],
            send_sem=xs_sem.at[t, way], recv_sem=xr_sem.at[t, way],
            device_id={"gx": gx + 1 - 2 * way}, device_id_type=MESH,
        )

    def y_copy(t, way):
        return pltpu.make_async_remote_copy(
            src_ref=ysend.at[t, way], dst_ref=yrecv.at[t, way],
            send_sem=ys_sem.at[t, way], recv_sem=yr_sem.at[t, way],
            device_id={"gy": gy + 1 - 2 * way}, device_id_type=MESH,
        )

    x_to, x_from = (has_right, has_left), (has_left, has_right)
    y_to, y_from = (has_high, has_low), (has_low, has_high)

    def send_x(t):
        for way in range(2):
            pl.when(x_to[way])(lambda: x_copy(t, way).start())

    def got_x(t):
        for way in range(2):
            pl.when(x_from[way])(lambda: x_copy(t, way).wait_recv())

    def y_rows(i, f, j):
        return pl.ds(f * 2 * CX + pl.multiple_of(i * 8, 8) + 2 * j, 2)

    def send_y(t):
        w = fields[t]

        def body(i, carry):
            for f in range(2):
                for j in range(4):
                    ysend[t, 0, y_rows(i, f, j), :] = w[f, EDGE + i * 4 + j, 6 + CY : 8 + CY, :]
                    ysend[t, 1, y_rows(i, f, j), :] = w[f, EDGE + i * 4 + j, 8:10, :]
            return carry

        lax.fori_loop(0, CX // 4, body, 0)
        for way in range(2):
            pl.when(y_to[way])(lambda: y_copy(t, way).start())

    def got_y(t):
        w = fields[t]
        for way in range(2):
            at = (6, 8 + CY)[way]

            def take(way=way, at=at):
                y_copy(t, way).wait_recv()

                def body(i, carry):
                    for f in range(2):
                        for j in range(4):
                            w[f, EDGE + i * 4 + j, at : at + 2, :] = yrecv[t, way, y_rows(i, f, j), :]
                    return carry

                lax.fori_loop(0, CX // 4, body, 0)

            pl.when(y_from[way])(take)

    targets = (
        (mate, 1, jnp.where(core == 0, band_b(chip), band_a(chip))),
        ({"shot": 2 * chip_a}, 2 + core, band_a(chip_a)),
        ({"shot": 2 * chip_b + 1}, 2 + core, band_b(chip_b)),
    )
    cuts = ((0, 8), (CX - 8, 8), (8, CX - 16))

    def m_copy(target):
        to, slot, _ = targets[target]
        return pltpu.make_async_remote_copy(
            src_ref=masks.at[0], dst_ref=masks.at[slot],
            send_sem=ms_sem.at[target], recv_sem=mr_sem.at[slot - 1],
            device_id=to, device_id_type=MESH,
        )

    def m_arrival(slot):
        return pltpu.make_async_copy(masks.at[slot], masks.at[slot], mr_sem.at[slot - 1])

    def band_rows(b):
        return pl.ds(pl.multiple_of(8 + BAND * b, 8), BAND)

    def e_copy(t, target, cut):
        to, slot, b = targets[target]
        at, n = cuts[cut]
        return pltpu.make_async_remote_copy(
            src_ref=fields[t].at[:, EDGE + at : EDGE + at + n, band_rows(b), :],
            dst_ref=bands.at[t - 1, slot, :, HALF + at : HALF + at + n],
            send_sem=es_sem.at[t - 1, target, cut], recv_sem=er_sem.at[t - 1, slot - 1, cut],
            device_id=to, device_id_type=MESH,
        )

    def e_arrival(t, slot, cut):
        at, n = cuts[cut]
        ref = bands.at[t - 1, slot, :, HALF + at : HALF + at + n]
        return pltpu.make_async_copy(ref, ref, er_sem.at[t - 1, slot - 1, cut])

    def e_own(t):
        return pltpu.make_async_copy(
            fields[t].at[:, EDGE : EDGE + CX, band_rows(band), :],
            bands.at[t - 1, 0, :, HALF : HALF + CX],
            es_sem.at[t - 1, 3, 0],
        )

    def send_e(t):
        e_own(t).start()
        for cut in range(3):
            for target in (1, 2, 0):
                e_copy(t, target, cut).start()

    def z_copy(t, way, f):
        here, there, n = (
            ((CX + 1, 1, HALF - 1), (CX, 0, HALF)),
            ((HALF, HALF + CX, HALF), (HALF, HALF + CX, HALF - 1)),
        )[way][f]
        return pltpu.make_async_remote_copy(
            src_ref=bands.at[t - 1, :, f, here : here + n],
            dst_ref=bands.at[t - 1, :, f, there : there + n],
            send_sem=zs_sem.at[t - 1, way, f], recv_sem=zr_sem.at[t - 1, way, f],
            device_id={"gx": gx + 1 - 2 * way}, device_id_type=MESH,
        )

    def send_z(t):
        e_own(t).wait()
        for slot in range(1, 4):
            for cut in range(2):
                e_arrival(t, slot, cut).wait()
        for way in range(2):
            for f in range(2):
                pl.when(x_to[way])(lambda: z_copy(t, way, f).start())

    lane = lax.broadcasted_iota(jnp.int32, (8, NZ), 1)
    near_up = jnp.where(lane < NZ - 1, NEAR, 0.0)
    near_down = jnp.where(lane > 0, NEAR, 0.0)
    far_up = jnp.where(lane < NZ - 2, FAR, 0.0)
    far_down = jnp.where(lane > 1, FAR, 0.0)
    spot = lax.broadcasted_iota(jnp.int32, (8, NZ), 0) * NZ + lane
    p = spos[0]
    lx = lax.shift_right_logical(p, 14) - gx * CX
    ly = (lax.shift_right_logical(p, 7) & 127) - gy * CY
    inside = (lx >= 0) & (lx < CX) & (ly >= 0) & (ly < CY)
    where = jnp.where(inside, (lx * CY + ly) * NZ + (p & 127), -1)

    def advance(t):
        w, new = fields[t], fields[t + 1]
        push = amp[0, t]

        def body(x, carry):
            X = x + EDGE
            for y in range(CY // 8):
                Y = 8 + 8 * y
                v = speed[x, 8 * y : 8 * y + 8, :]
                for f in range(2):
                    c = w[f, X, Y : Y + 8, :]
                    lap = CENTRE * c
                    lap = lap + NEAR * (w[f, X + 1, Y : Y + 8, :] + w[f, X - 1, Y : Y + 8, :])
                    lap = lap + FAR * (w[f, X + 2, Y : Y + 8, :] + w[f, X - 2, Y : Y + 8, :])
                    lap = lap + NEAR * (w[f, X, Y + 1 : Y + 9, :] + w[f, X, Y - 1 : Y + 7, :])
                    lap = lap + FAR * (w[f, X, Y + 2 : Y + 10, :] + w[f, X, Y - 2 : Y + 6, :])
                    lap = lap + near_up * pltpu.roll(c, NZ - 1, 1) + near_down * pltpu.roll(c, 1, 1)
                    lap = lap + far_up * pltpu.roll(c, NZ - 2, 1) + far_down * pltpu.roll(c, 2, 1)
                    if t == 0:
                        before = old[f, x, 8 * y : 8 * y + 8, :]
                    else:
                        before = fields[t - 1][f, X, Y : Y + 8, :]
                    value = 2.0 * c - before + v * lap
                    if f == 0:
                        add = jnp.where(spot == where - (x * CY + 8 * y) * NZ, push, 0.0)
                    else:
                        add = drive[t, pl.ds(pl.multiple_of(x * CY + 8 * y, 8), 8), :]
                    new[f, X, Y : Y + 8, :] = value + add
            return carry

        lax.fori_loop(0, CX, body, 0)

    for copy in loads[:2]:
        copy.wait()
    pl.semaphore_wait(barrier, TILES - 1 + len(peers))
    send_x(0)
    send_y(0)
    for target in range(3):
        m_copy(target).start()
    for copy in loads[2:]:
        copy.wait()
    table.wait()
    for t in range(STEPS):
        got_x(t)
        got_y(t)
        advance(t)
        if t + 1 < STEPS:
            send_x(t + 1)
            send_y(t + 1)
        send_e(t + 1)
        if t:
            send_z(t)
    stores = [
        pltpu.make_async_copy(w3.at[(f,) + inner], (s_out, r_out)[f].at[0], out_sem.at[f]) for f in range(2)
    ]
    for copy in stores:
        copy.start()
    send_z(STEPS)
    for slot in range(1, 4):
        m_arrival(slot).wait()
    for t in range(1, STEPS + 1):
        for slot in range(1, 4):
            e_arrival(t, slot, 2).wait()
    for t in range(1, STEPS + 1):
        for way in range(2):
            for f in range(2):
                pl.when(x_from[way])(lambda: z_copy(t, way, f).wait_recv())

    dxs = (2, 1, 3, 0)
    dzs = (4, 3, 5, 2, 6, 1, 7, 0)

    def to_whom(group, i):
        dx = jnp.int32(dxs[0])
        for g in range(1, GROUPS):
            dx = jnp.where(group == g, dxs[g], dx)
        dz = jnp.int32(dzs[0])
        for j in range(1, SG):
            dz = jnp.where(i == j, dzs[j], dz)
        return lax.rem(gx + dz, N_GX), lax.rem(gy + dx, N_GY)

    place = []
    for c in range(CHIPS):
        at = jnp.where(c == chip, 0, jnp.where(c == first, 1, jnp.where(c == second, 2, 3)))
        place.append(at)

    def correlate(group):
        def body(i, carry):
            ox, oy = to_whom(group, i)
            k = jnp.clip(strip[ox * N_GY + oy, 0], 0, CX - 1)
            m = [masks[s] for s in range(4)]
            for h in range(OFFS):
                total = None
                for s in range(4):
                    one = None
                    for t in range(STEPS):
                        term = bands[t, s, 0, k + OFFS - h] * bands[t, s, 1, k + h]
                        one = term if one is None else one + term
                    one = one * m[s]
                    total = one if total is None else total + one
                part[group, place[h // 4], i, h % 4] = total
            return carry

        lax.fori_loop(0, SG, body, 0)

    def b_copy(group):
        return pltpu.make_async_remote_copy(
            src_ref=part.at[group, 2:4], dst_ref=half.at[group],
            send_sem=bs_sem.at[group], recv_sem=br_sem.at[group],
            device_id={"shot": 2 * second + core}, device_id_type=MESH,
        )

    def strips(group):
        return pl.ds(group * SG, SG)

    def out_rows(b):
        return pl.ds(pl.multiple_of(BAND * b, 8), BAND)

    homes = ((mate, 0, 0, 2 * (1 - core)), ({"shot": 2 * first}, 1 + core, 1, 0), ({"shot": 2 * first + 1}, 1 + core, 1, 2))

    def c_copy(group, home):
        to, slot, at, h = homes[home]
        return pltpu.make_async_remote_copy(
            src_ref=part.at[group, at, :, pl.ds(h, 2)],
            dst_ref=final.at[strips(group), :, out_rows(band), :],
            send_sem=cs_sem.at[group, home], recv_sem=cr_sem.at[group, slot],
            device_id=to, device_id_type=MESH,
        )

    sources = (targets[0][2], band_a(chip_a), band_b(chip_b))

    def c_arrival(group, slot):
        ref = final.at[strips(group), :, out_rows(sources[slot]), :]
        return pltpu.make_async_copy(ref, ref, cr_sem.at[group, slot])

    def d_copy(group, i):
        ox, oy = to_whom(group, i)
        return pltpu.make_async_remote_copy(
            src_ref=final.at[group * SG + i], dst_ref=g_out.at[0, :, tile, 0],
            send_sem=d_sem.at[0], recv_sem=d_sem.at[1],
            device_id={"gx": ox, "gy": oy}, device_id_type=MESH,
        )

    def own_copy():
        return pltpu.make_async_copy(final.at[TILES - 1], g_out.at[0, :, tile, 0], d_sem.at[2])

    def from_second(group):
        b_copy(group).wait_recv()

        def body(i, carry):
            for at in (1, 0):
                part[group, at, i] = part[group, at, i] + half[group, at, i]
            return carry

        lax.fori_loop(0, SG, body, 0)
        for home in (1, 2, 0):
            c_copy(group, home).start()

        def keep(i, carry):
            final[group * SG + i, :, out_rows(band), :] = part[group, 0, i, pl.ds(2 * core, 2)]
            return carry

        lax.fori_loop(0, SG, keep, 0)

    def from_first(group):
        for slot in range(3):
            c_arrival(group, slot).wait()

        def body(i, carry):
            mine = (group == GROUPS - 1) & (i == SG - 1)

            @pl.when(mine)
            def _():
                own_copy().start()

            @pl.when(jnp.logical_not(mine))
            def _():
                d_copy(group, i).start()

            return carry

        lax.fori_loop(0, SG, body, 0)

    def stage(it, carry):
        @pl.when(it < GROUPS)
        def _():
            correlate(it)
            b_copy(it).start()

        @pl.when((it >= 1) & (it < GROUPS + 1))
        def _():
            from_second(it - 1)

        @pl.when(it >= 2)
        def _():
            from_first(it - 2)

        return carry

    lax.fori_loop(0, GROUPS + 2, stage, 0)

    for t in range(STEPS):
        for way in range(2):
            pl.when(x_to[way])(lambda: x_copy(t, way).wait_send())
            pl.when(y_to[way])(lambda: y_copy(t, way).wait_send())
            for f in range(2):
                pl.when(x_to[way])(lambda: z_copy(t + 1, way, f).wait_send())
        for target in range(3):
            for cut in range(3):
                e_copy(t + 1, target, cut).wait_send()
    for target in range(3):
        m_copy(target).wait_send()

    def drain(group, carry):
        b_copy(group).wait_send()
        for home in range(3):
            c_copy(group, home).wait_send()
        return carry

    lax.fori_loop(0, GROUPS, drain, 0)
    for copy in stores:
        copy.wait()
    own_copy().wait()
    sent = final.at[0 : TILES - 1]
    pltpu.make_async_copy(sent, sent, d_sem.at[0]).wait()
    arrived = g_out.at[0, :, 0 : TILES - 1, 0]
    pltpu.make_async_copy(arrived, arrived, d_sem.at[1]).wait()


def body(vel_coef, src_prev, src_cur, rcv_prev, rcv_cur, src_pos, src_amp, rcv_pos, rcv_data, aperture, owner):
    big = [
        pltpu.with_memory_space_constraint(v, pltpu.HBM)
        for v in (vel_coef, src_prev, src_cur, rcv_prev, rcv_cur)
    ]
    whole = pl.BlockSpec(memory_space=pl.ANY)
    vmem = pl.BlockSpec(memory_space=pltpu.VMEM)
    smem = pl.BlockSpec(memory_space=pltpu.SMEM)
    DMA = pltpu.SemaphoreType.DMA
    wave = pltpu.VMEM((2, CX + 2 * EDGE, CY + 16, NZ), F32)
    return pl.pallas_call(
        main_kernel,
        out_shape=(
            jax.ShapeDtypeStruct(src_cur.shape, F32),
            jax.ShapeDtypeStruct(rcv_cur.shape, F32),
            jax.ShapeDtypeStruct((1, 2, TILES, 1, CY, NZ), F32),
        ),
        in_specs=[pl.BlockSpec(memory_space=pltpu.HBM)] * 5 + [vmem] * 4 + [smem] * 2,
        out_specs=(whole, whole, whole),
        scratch_shapes=[
            wave, wave, wave, wave,
            pltpu.VMEM((STEPS, 4, 2, EXT, BAND, NZ), F32),
            pltpu.VMEM((2, CX, CY, NZ), F32),
            pltpu.VMEM((CX, CY, NZ), F32),
            pltpu.VMEM((STEPS, CX * CY, NZ), F32),
            pltpu.VMEM((STEPS, 2, 4 * CX, NZ), F32),
            pltpu.VMEM((STEPS, 2, 4 * CX, NZ), F32),
            pltpu.VMEM((GROUPS, CHIPS, SG, 4, BAND, NZ), F32),
            pltpu.VMEM((GROUPS, 2, SG, 4, BAND, NZ), F32),
            pltpu.VMEM((TILES, 2, CY, NZ), F32),
            pltpu.VMEM((4, 8, NZ), F32),
            pltpu.VMEM((TILES, NZ), jnp.int32),
            pltpu.SMEM((TILES, NZ), jnp.int32),
            DMA((6,)),
            DMA((STEPS, 2)), DMA((STEPS, 2)), DMA((STEPS, 2)), DMA((STEPS, 2)),
            DMA((3,)), DMA((3,)),
            DMA((STEPS, 4, 3)), DMA((STEPS, 3, 3)),
            DMA((STEPS, 2, 2)), DMA((STEPS, 2, 2)),
            DMA((GROUPS,)), DMA((GROUPS,)),
            DMA((GROUPS, 3)), DMA((GROUPS, 3)),
            DMA((3,)), DMA((2,)),
        ],
        compiler_params=pltpu.CompilerParams(
            collective_id=0, has_side_effects=True, vmem_limit_bytes=48 * 1024 * 1024
        ),
        name="migrate",
    )(*big, rcv_pos, jnp.transpose(rcv_data, (1, 0, 2)), aperture, owner, src_pos, src_amp)


def solution(mesh):
    return jax.shard_map(
        body,
        mesh=mesh,
        in_specs=(
            P("gx", "gy", None),
            P("shot", "gx", "gy", None),
            P("shot", "gx", "gy", None),
            P("shot", "gx", "gy", None),
            P("shot", "gx", "gy", None),
            P("shot"),
            P("shot", None),
            P("shot", None),
            P("shot", None, None),
            P("shot", None),
            P(),
        ),
        out_specs=(
            P("shot", "gx", "gy", None),
            P("shot", "gx", "gy", None),
            P(("gx", "gy"), "shot", None, None, None, None),
        ),
        check_vma=False,
    )
```

```python
import jax
import jax.numpy as jnp
from jax import lax
from jax.experimental import pallas as pl
from jax.experimental.pallas import tpu as pltpu
from jax.sharding import PartitionSpec as P

MESH = pl.DeviceIdType.MESH
OFFS = 16
STEPS = 3
HALF = 8
NEAR = 4.0 / 3.0
FAR = -1.0 / 12.0
CENTRE = 3.0 * -2.5

CX, CY, NZ = 32, 32, 128
N_GX, N_GY, N_SHOT = 8, 4, 8
TILES = N_GX * N_GY
GROUPS = 8
SG = TILES // GROUPS
CHIPS = N_SHOT // 2
UN = 7
EDGE = 2
EXT = CX + 2 * HALF
BAND = 8
F32 = jnp.float32


def main_kernel(
    vel, s_prev, s_cur, r_prev, r_cur, pos_in, data_in, ap_in, owner_in, amp_in, spos,
    s_out, r_out, g_out,
    w0, w1, w2, w3, bands, old, speed, drive, ysend, yrecv, part, half, final, masks, strip_v, strip,
    pos_ref, data_ref, ap_ref, owner_ref, amp,
    load_sem, xs_sem, xr_sem, ys_sem, yr_sem, ms_sem, mr_sem, es_sem, er_sem, zs_sem, zr_sem,
    bs_sem, br_sem, cs_sem, cr_sem, d_sem, out_sem,
):
    gx, gy, shot = lax.axis_index("gx"), lax.axis_index("gy"), lax.axis_index("shot")
    core = lax.rem(shot, 2)
    chip = lax.div(shot, 2)
    tile = gx * N_GY + gy
    fields = (w0, w1, w2, w3)
    has_left, has_right = gx > 0, gx < N_GX - 1
    has_low, has_high = gy > 0, gy < N_GY - 1

    def pair_a(c):
        return c + 1 - 2 * lax.rem(c, 2)

    def pair_b(c):
        return CHIPS - 1 - c

    def band_a(c):
        return lax.rem(lax.div(c + 1, 2), 2)

    def band_b(c):
        return 2 + lax.div(c, 2)

    chip_a, chip_b = pair_a(chip), pair_b(chip)
    first = jnp.where(core == 0, chip_a, chip_b)
    second = jnp.where(core == 0, chip_b, chip_a)
    band = jnp.where(core == 0, band_a(chip), band_b(chip))
    mate = {"shot": shot + 1 - 2 * core}
    peers = (mate, {"shot": 2 * chip_a}, {"shot": 2 * chip_a + 1}, {"shot": 2 * chip_b}, {"shot": 2 * chip_b + 1})

    barrier = pltpu.get_barrier_semaphore()
    for peer in peers:
        pl.semaphore_signal(barrier, inc=1, device_id=peer, device_id_type=MESH)

    def greet(j, carry):
        peer = lax.rem(tile + j, TILES)
        pl.semaphore_signal(
            barrier, inc=1, device_id={"gx": lax.div(peer, N_GY), "gy": lax.rem(peer, N_GY)},
            device_id_type=MESH,
        )
        return carry

    lax.fori_loop(1, TILES, greet, 0)

    inner = (slice(EDGE, EDGE + CX), slice(8, 8 + CY))
    loads = [
        pltpu.make_async_copy(s_cur.at[0], w0.at[(0,) + inner], load_sem.at[0]),
        pltpu.make_async_copy(r_cur.at[0], w0.at[(1,) + inner], load_sem.at[1]),
        pltpu.make_async_copy(s_prev.at[0], old.at[0], load_sem.at[2]),
        pltpu.make_async_copy(r_prev.at[0], old.at[1], load_sem.at[3]),
        pltpu.make_async_copy(vel, speed, load_sem.at[4]),
    ]
    small = [
        pltpu.make_async_copy(a, b, load_sem.at[6 + i])
        for i, (a, b) in enumerate(
            ((owner_in, owner_ref), (ap_in, ap_ref), (pos_in, pos_ref), (data_in, data_ref), (amp_in, amp))
        )
    ]
    for copy in small + loads:
        copy.start()
    for copy in small:
        copy.wait()

    row = owner_ref[pl.ds(tile, 1), :]
    match = row == lax.broadcasted_iota(jnp.int32, (TILES, TILES), 0)
    number = lax.broadcasted_iota(jnp.int32, (TILES, TILES), 1)
    found = jnp.max(jnp.where(match, number, 0), axis=1, keepdims=True)
    strip_v[...] = jnp.broadcast_to(found, (TILES, NZ))
    table = pltpu.make_async_copy(strip_v, strip, load_sem.at[5])
    table.start()
    hit = jnp.max(jnp.where(ap_ref[...] == tile, 1.0, 0.0), axis=1, keepdims=True)
    masks[0] = jnp.broadcast_to(hit, (8, NZ))

    def clear_x(at, wide):
        def body(i, carry):
            for w in fields[:STEPS]:
                for f in range(2):
                    w[f, at + i, 8 : 8 + CY, :] = jnp.zeros((CY, NZ), F32)
            return carry

        lax.fori_loop(0, EDGE, body, 0)

        def body2(i, carry):
            for t in range(STEPS):
                for s in range(4):
                    for f in range(2):
                        bands[t, s, f, wide + i] = jnp.zeros((BAND, NZ), F32)
            return carry

        lax.fori_loop(0, HALF, body2, 0)

    def clear_y(at):
        def body(i, carry):
            for w in fields[:STEPS]:
                for f in range(2):
                    w[f, EDGE + i, at : at + 8, :] = jnp.zeros((8, NZ), F32)
            return carry

        lax.fori_loop(0, CX, body, 0)

    pl.when(jnp.logical_not(has_left))(lambda: clear_x(0, 0))
    pl.when(jnp.logical_not(has_right))(lambda: clear_x(EDGE + CX, HALF + CX))
    pl.when(jnp.logical_not(has_low))(lambda: clear_y(0))
    pl.when(jnp.logical_not(has_high))(lambda: clear_y(8 + CY))

    def inject():
        pos = pos_ref[...]
        rx = lax.shift_right_logical(pos, 14) - gx * CX
        ry = (lax.shift_right_logical(pos, 7) & 127) - gy * CY
        ok = (rx >= 0) & (rx < CX) & (ry >= 0) & (ry < CY)
        cell = jnp.where(ok, rx * CY + ry, -1)
        n = pos.shape[1]
        depth = lax.broadcasted_iota(jnp.int32, (NZ, n), 0) == (pos & 127)
        parts = [[], [], []]
        for t in range(STEPS):
            left = jnp.where(depth, data_ref[t], 0.0)
            for piece in parts:
                cut = left.astype(jnp.bfloat16)
                piece.append(cut)
                left = left - cut.astype(F32)
        parts = [jnp.concatenate(piece, axis=0) for piece in parts]
        rows = 256
        for at in range(0, CX * CY, rows):
            spot = lax.broadcasted_iota(jnp.int32, (rows, n), 0) + at == cell
            spot = jnp.where(spot, 1.0, 0.0).astype(jnp.bfloat16)
            total = None
            for piece in parts:
                term = lax.dot_general(spot, piece, (((1,), (1,)), ((), ())), preferred_element_type=F32)
                total = term if total is None else total + term
            for t in range(STEPS):
                drive[t, at : at + rows, :] = total[:, t * NZ : (t + 1) * NZ]

    inject()

    def x_copy(t, way):
        here, there = ((CX, 0), (EDGE, EDGE + CX))[way]
        return pltpu.make_async_remote_copy(
            src_ref=fields[t].at[:, here : here + EDGE, 8 : 8 + CY, :],
            dst_ref=fields[t].at[:, there : there + EDGE, 8 : 8 + CY, :],
            send_sem=xs_sem.at[t, way], recv_sem=xr_sem.at[t, way],
            device_id={"gx": gx + 1 - 2 * way}, device_id_type=MESH,
        )

    def y_copy(t, way):
        return pltpu.make_async_remote_copy(
            src_ref=ysend.at[t, way], dst_ref=yrecv.at[t, way],
            send_sem=ys_sem.at[t, way], recv_sem=yr_sem.at[t, way],
            device_id={"gy": gy + 1 - 2 * way}, device_id_type=MESH,
        )

    x_to, x_from = (has_right, has_left), (has_left, has_right)
    y_to, y_from = (has_high, has_low), (has_low, has_high)

    def send_x(t):
        for way in range(2):
            pl.when(x_to[way])(lambda: x_copy(t, way).start())

    def got_x(t):
        for way in range(2):
            pl.when(x_from[way])(lambda: x_copy(t, way).wait_recv())

    def y_rows(i, f, j):
        return pl.ds(f * 2 * CX + pl.multiple_of(i * 8, 8) + 2 * j, 2)

    def send_y(t):
        w = fields[t]

        def body(i, carry):
            for f in range(2):
                for j in range(4):
                    ysend[t, 0, y_rows(i, f, j), :] = w[f, EDGE + i * 4 + j, 6 + CY : 8 + CY, :]
                    ysend[t, 1, y_rows(i, f, j), :] = w[f, EDGE + i * 4 + j, 8:10, :]
            return carry

        lax.fori_loop(0, CX // 4, body, 0)
        for way in range(2):
            pl.when(y_to[way])(lambda: y_copy(t, way).start())

    def got_y(t):
        w = fields[t]
        for way in range(2):
            at = (6, 8 + CY)[way]

            def take(way=way, at=at):
                y_copy(t, way).wait_recv()

                def body(i, carry):
                    for f in range(2):
                        for j in range(4):
                            w[f, EDGE + i * 4 + j, at : at + 2, :] = yrecv[t, way, y_rows(i, f, j), :]
                    return carry

                lax.fori_loop(0, CX // 4, body, 0)

            pl.when(y_from[way])(take)

    targets = (
        (mate, 1, jnp.where(core == 0, band_b(chip), band_a(chip))),
        ({"shot": 2 * chip_a}, 2 + core, band_a(chip_a)),
        ({"shot": 2 * chip_b + 1}, 2 + core, band_b(chip_b)),
    )
    cuts = ((0, 8), (CX - 8, 8), (8, CX - 16))

    def m_copy(target):
        to, slot, _ = targets[target]
        return pltpu.make_async_remote_copy(
            src_ref=masks.at[0], dst_ref=masks.at[slot],
            send_sem=ms_sem.at[target], recv_sem=mr_sem.at[slot - 1],
            device_id=to, device_id_type=MESH,
        )

    def m_arrival(slot):
        return pltpu.make_async_copy(masks.at[slot], masks.at[slot], mr_sem.at[slot - 1])

    def band_rows(b):
        return pl.ds(pl.multiple_of(8 + BAND * b, 8), BAND)

    def e_copy(t, target, cut):
        to, slot, b = targets[target]
        at, n = cuts[cut]
        return pltpu.make_async_remote_copy(
            src_ref=fields[t].at[:, EDGE + at : EDGE + at + n, band_rows(b), :],
            dst_ref=bands.at[t - 1, slot, :, HALF + at : HALF + at + n],
            send_sem=es_sem.at[t - 1, target, cut], recv_sem=er_sem.at[t - 1, slot - 1, cut],
            device_id=to, device_id_type=MESH,
        )

    def e_arrival(t, slot, cut):
        at, n = cuts[cut]
        ref = bands.at[t - 1, slot, :, HALF + at : HALF + at + n]
        return pltpu.make_async_copy(ref, ref, er_sem.at[t - 1, slot - 1, cut])

    def e_own(t):
        return pltpu.make_async_copy(
            fields[t].at[:, EDGE : EDGE + CX, band_rows(band), :],
            bands.at[t - 1, 0, :, HALF : HALF + CX],
            es_sem.at[t - 1, 3, 0],
        )

    def send_e(t):
        e_own(t).start()
        for cut in range(3):
            for target in (1, 2, 0):
                e_copy(t, target, cut).start()

    def z_copy(t, way, f):
        here, there, n = (
            ((CX + 1, 1, HALF - 1), (CX, 0, HALF)),
            ((HALF, HALF + CX, HALF), (HALF, HALF + CX, HALF - 1)),
        )[way][f]
        return pltpu.make_async_remote_copy(
            src_ref=bands.at[t - 1, :, f, here : here + n],
            dst_ref=bands.at[t - 1, :, f, there : there + n],
            send_sem=zs_sem.at[t - 1, way, f], recv_sem=zr_sem.at[t - 1, way, f],
            device_id={"gx": gx + 1 - 2 * way}, device_id_type=MESH,
        )

    def send_z(t):
        e_own(t).wait()
        for slot in range(1, 4):
            for cut in range(2):
                e_arrival(t, slot, cut).wait()
        for way in range(2):
            for f in range(2):
                pl.when(x_to[way])(lambda: z_copy(t, way, f).start())

    lane = lax.broadcasted_iota(jnp.int32, (8, NZ), 1)
    near_up = jnp.where(lane < NZ - 1, NEAR, 0.0)
    near_down = jnp.where(lane > 0, NEAR, 0.0)
    far_up = jnp.where(lane < NZ - 2, FAR, 0.0)
    far_down = jnp.where(lane > 1, FAR, 0.0)
    spot = lax.broadcasted_iota(jnp.int32, (8, NZ), 0) * NZ + lane
    p = spos[0]
    lx = lax.shift_right_logical(p, 14) - gx * CX
    ly = (lax.shift_right_logical(p, 7) & 127) - gy * CY
    within = (lx >= 0) & (lx < CX) & (ly >= 0) & (ly < CY)
    where = jnp.where(within, (lx * CY + ly) * NZ + (p & 127), -1)

    def cells(t, x, ys):
        w, new = fields[t], fields[t + 1]
        X = x + EDGE
        for y in ys:
            Y = 8 + 8 * y
            v = speed[x, 8 * y : 8 * y + 8, :]
            for f in range(2):
                c = w[f, X, Y : Y + 8, :]
                near = (w[f, X + 1, Y : Y + 8, :] + w[f, X - 1, Y : Y + 8, :]) + (
                    w[f, X, Y + 1 : Y + 9, :] + w[f, X, Y - 1 : Y + 7, :]
                )
                far = (w[f, X + 2, Y : Y + 8, :] + w[f, X - 2, Y : Y + 8, :]) + (
                    w[f, X, Y + 2 : Y + 10, :] + w[f, X, Y - 2 : Y + 6, :]
                )
                lap = CENTRE * c + NEAR * near + FAR * far
                lap = lap + (near_up * pltpu.roll(c, NZ - 1, 1) + near_down * pltpu.roll(c, 1, 1))
                lap = lap + (far_up * pltpu.roll(c, NZ - 2, 1) + far_down * pltpu.roll(c, 2, 1))
                if t == 0:
                    before = old[f, x, 8 * y : 8 * y + 8, :]
                else:
                    before = fields[t - 1][f, X, Y : Y + 8, :]
                value = (2.0 * c - before) + v * lap
                if f == 0:
                    add = jnp.where(spot == where - (x * CY + 8 * y) * NZ, amp[0, t], 0.0)
                else:
                    add = drive[t, pl.ds(pl.multiple_of(x * CY + 8 * y, 8), 8), :]
                new[f, X, Y : Y + 8, :] = value + add

    def inside_cells(t):
        def body(i, carry):
            for j in range(UN):
                cells(t, EDGE + UN * i + j, (1, 2))
            return carry

        lax.fori_loop(0, (CX - 2 * EDGE) // UN, body, 0)

    def rim_cells(t):
        def body(i, carry):
            for j in range(UN):
                cells(t, EDGE + UN * i + j, (0, 3))
            return carry

        def ends(i, carry):
            cells(t, i + jnp.where(i >= EDGE, CX - 2 * EDGE, 0), (0, 1, 2, 3))
            return carry

        lax.fori_loop(0, 2 * EDGE, ends, 0)
        lax.fori_loop(0, (CX - 2 * EDGE) // UN, body, 0)

    for copy in loads[:2]:
        copy.wait()
    pl.semaphore_wait(barrier, TILES - 1 + len(peers))
    send_x(0)
    send_y(0)
    for target in range(3):
        m_copy(target).start()
    for copy in loads[2:]:
        copy.wait()
    table.wait()
    for t in range(STEPS):
        inside_cells(t)
        got_x(t)
        got_y(t)
        rim_cells(t)
        if t + 1 < STEPS:
            send_x(t + 1)
            send_y(t + 1)
        send_e(t + 1)
        if t:
            send_z(t)
    stores = [
        pltpu.make_async_copy(w3.at[(f,) + inner], (s_out, r_out)[f].at[0], out_sem.at[f]) for f in range(2)
    ]
    for copy in stores:
        copy.start()
    send_z(STEPS)
    for slot in range(1, 4):
        m_arrival(slot).wait()
    for t in range(1, STEPS + 1):
        for slot in range(1, 4):
            e_arrival(t, slot, 2).wait()
    for t in range(1, STEPS + 1):
        for way in range(2):
            for f in range(2):
                pl.when(x_from[way])(lambda: z_copy(t, way, f).wait_recv())

    dxs = (2, 1, 3, 0)
    dzs = ((3, 5, 1, 7), (4, 2, 6, 0))

    def to_whom(group, i):
        dx = jnp.int32(dxs[0])
        for g in range(1, N_GY):
            dx = jnp.where(lax.div(group, 2) == g, dxs[g], dx)
        dz = jnp.int32(dzs[0][0])
        for g in range(2):
            for j in range(SG):
                dz = jnp.where((lax.rem(group, 2) == g) & (i == j), dzs[g][j], dz)
        return lax.rem(gx + dz, N_GX), lax.rem(gy + dx, N_GY)

    place = []
    for c in range(CHIPS):
        at = jnp.where(c == chip, 0, jnp.where(c == first, 1, jnp.where(c == second, 2, 3)))
        place.append(at)

    def correlate(group):
        def body(i, carry):
            ox, oy = to_whom(group, i)
            k = jnp.clip(strip[ox * N_GY + oy, 0], 0, CX - 1)
            m = [masks[s] for s in range(4)]
            for h in range(OFFS):
                total = None
                for s in range(4):
                    one = None
                    for t in range(STEPS):
                        term = bands[t, s, 0, k + OFFS - h] * bands[t, s, 1, k + h]
                        one = term if one is None else one + term
                    one = one * m[s]
                    total = one if total is None else total + one
                part[group, place[h // 4], i, h % 4] = total
            return carry

        lax.fori_loop(0, SG, body, 0)

    def b_copy(group):
        return pltpu.make_async_remote_copy(
            src_ref=part.at[group, 2:4], dst_ref=half.at[group],
            send_sem=bs_sem.at[group], recv_sem=br_sem.at[group],
            device_id={"shot": 2 * second + core}, device_id_type=MESH,
        )

    def strips(group):
        return pl.ds(group * SG, SG)

    def out_rows(b):
        return pl.ds(pl.multiple_of(BAND * b, 8), BAND)

    homes = ((mate, 0, 0, 2 * (1 - core)), ({"shot": 2 * first}, 1 + core, 1, 0), ({"shot": 2 * first + 1}, 1 + core, 1, 2))

    def c_copy(group, home):
        to, slot, at, h = homes[home]
        return pltpu.make_async_remote_copy(
            src_ref=part.at[group, at, :, pl.ds(h, 2)],
            dst_ref=final.at[strips(group), :, out_rows(band), :],
            send_sem=cs_sem.at[group, home], recv_sem=cr_sem.at[group, slot],
            device_id=to, device_id_type=MESH,
        )

    sources = (targets[0][2], band_a(chip_a), band_b(chip_b))

    def c_arrival(group, slot):
        ref = final.at[strips(group), :, out_rows(sources[slot]), :]
        return pltpu.make_async_copy(ref, ref, cr_sem.at[group, slot])

    def d_copy(group, i):
        ox, oy = to_whom(group, i)
        return pltpu.make_async_remote_copy(
            src_ref=final.at[group * SG + i], dst_ref=g_out.at[0, :, tile, 0],
            send_sem=d_sem.at[0], recv_sem=d_sem.at[1],
            device_id={"gx": ox, "gy": oy}, device_id_type=MESH,
        )

    def own_copy():
        return pltpu.make_async_copy(final.at[TILES - 1], g_out.at[0, :, tile, 0], d_sem.at[2])

    def from_second(group):
        b_copy(group).wait_recv()

        def body(i, carry):
            for at in (1, 0):
                part[group, at, i] = part[group, at, i] + half[group, at, i]
            return carry

        lax.fori_loop(0, SG, body, 0)
        for home in (1, 2, 0):
            c_copy(group, home).start()

        def keep(i, carry):
            final[group * SG + i, :, out_rows(band), :] = part[group, 0, i, pl.ds(2 * core, 2)]
            return carry

        lax.fori_loop(0, SG, keep, 0)

    def from_first(group):
        for slot in range(3):
            c_arrival(group, slot).wait()

        def body(i, carry):
            mine = (group == GROUPS - 1) & (i == SG - 1)

            @pl.when(mine)
            def _():
                own_copy().start()

            @pl.when(jnp.logical_not(mine))
            def _():
                d_copy(group, i).start()

            return carry

        lax.fori_loop(0, SG, body, 0)

    def stage(it, carry):
        @pl.when(it < GROUPS)
        def _():
            correlate(it)
            b_copy(it).start()

        @pl.when((it >= 1) & (it < GROUPS + 1))
        def _():
            from_second(it - 1)

        @pl.when(it >= 2)
        def _():
            from_first(it - 2)

        return carry

    lax.fori_loop(0, GROUPS + 2, stage, 0)

    for t in range(STEPS):
        for way in range(2):
            pl.when(x_to[way])(lambda: x_copy(t, way).wait_send())
            pl.when(y_to[way])(lambda: y_copy(t, way).wait_send())
            for f in range(2):
                pl.when(x_to[way])(lambda: z_copy(t + 1, way, f).wait_send())
        for target in range(3):
            for cut in range(3):
                e_copy(t + 1, target, cut).wait_send()
    for target in range(3):
        m_copy(target).wait_send()

    def drain(group, carry):
        b_copy(group).wait_send()
        for home in range(3):
            c_copy(group, home).wait_send()
        return carry

    lax.fori_loop(0, GROUPS, drain, 0)
    for copy in stores:
        copy.wait()
    own_copy().wait()
    sent = final.at[0 : TILES - 1]
    pltpu.make_async_copy(sent, sent, d_sem.at[0]).wait()
    arrived = g_out.at[0, :, 0 : TILES - 1, 0]
    pltpu.make_async_copy(arrived, arrived, d_sem.at[1]).wait()


def hand_over_kernel(a, b, c, x, y, z, sem):
    copies = [pltpu.make_async_copy(v, w, sem.at[i]) for i, (v, w) in enumerate(((a, x), (b, y), (c, z)))]
    for copy in copies:
        copy.start()
    for copy in copies:
        copy.wait()


def body(vel_coef, src_prev, src_cur, rcv_prev, rcv_cur, src_pos, src_amp, rcv_pos, rcv_data, aperture, owner):
    big = [
        pltpu.with_memory_space_constraint(v, pltpu.HBM)
        for v in (
            vel_coef, src_prev, src_cur, rcv_prev, rcv_cur,
            rcv_pos, jnp.transpose(rcv_data, (1, 0, 2)), aperture, owner, src_amp,
        )
    ]
    whole = pl.BlockSpec(memory_space=pl.ANY)
    DMA = pltpu.SemaphoreType.DMA
    wave = pltpu.VMEM((2, CX + 2 * EDGE, CY + 16, NZ), F32)
    done = pl.pallas_call(
        main_kernel,
        out_shape=(
            jax.ShapeDtypeStruct(src_cur.shape, F32),
            jax.ShapeDtypeStruct(rcv_cur.shape, F32),
            jax.ShapeDtypeStruct((1, 2, TILES, 1, CY, NZ), F32),
        ),
        in_specs=[pl.BlockSpec(memory_space=pltpu.HBM)] * 10 + [pl.BlockSpec(memory_space=pltpu.SMEM)],
        out_specs=(whole, whole, whole),
        scratch_shapes=[
            wave, wave, wave, wave,
            pltpu.VMEM((STEPS, 4, 2, EXT, BAND, NZ), F32),
            pltpu.VMEM((2, CX, CY, NZ), F32),
            pltpu.VMEM((CX, CY, NZ), F32),
            pltpu.VMEM((STEPS, CX * CY, NZ), F32),
            pltpu.VMEM((STEPS, 2, 4 * CX, NZ), F32),
            pltpu.VMEM((STEPS, 2, 4 * CX, NZ), F32),
            pltpu.VMEM((GROUPS, CHIPS, SG, 4, BAND, NZ), F32),
            pltpu.VMEM((GROUPS, 2, SG, 4, BAND, NZ), F32),
            pltpu.VMEM((TILES, 2, CY, NZ), F32),
            pltpu.VMEM((4, 8, NZ), F32),
            pltpu.VMEM((TILES, NZ), jnp.int32),
            pltpu.SMEM((TILES, NZ), jnp.int32),
            pltpu.VMEM(rcv_pos.shape, jnp.int32),
            pltpu.VMEM((STEPS, 1, rcv_pos.shape[1]), F32),
            pltpu.VMEM(aperture.shape, jnp.int32),
            pltpu.VMEM(owner.shape, jnp.int32),
            pltpu.SMEM(src_amp.shape, F32),
            DMA((12,)),
            DMA((STEPS, 2)), DMA((STEPS, 2)), DMA((STEPS, 2)), DMA((STEPS, 2)),
            DMA((3,)), DMA((3,)),
            DMA((STEPS, 4, 3)), DMA((STEPS, 3, 3)),
            DMA((STEPS, 2, 2)), DMA((STEPS, 2, 2)),
            DMA((GROUPS,)), DMA((GROUPS,)),
            DMA((GROUPS, 3)), DMA((GROUPS, 3)),
            DMA((3,)), DMA((2,)),
        ],
        compiler_params=pltpu.CompilerParams(
            collective_id=0, has_side_effects=True, vmem_limit_bytes=48 * 1024 * 1024
        ),
        name="migrate",
    )(*big, src_pos)
    return pl.pallas_call(
        hand_over_kernel,
        out_shape=tuple(jax.ShapeDtypeStruct(v.shape, v.dtype) for v in done),
        in_specs=[whole] * 3,
        out_specs=(whole,) * 3,
        scratch_shapes=[DMA((3,))],
        compiler_params=pltpu.CompilerParams(vmem_limit_bytes=1024 * 1024),
        name="hand_over",
    )(*done)


def solution(mesh):
    return jax.shard_map(
        body,
        mesh=mesh,
        in_specs=(
            P("gx", "gy", None),
            P("shot", "gx", "gy", None),
            P("shot", "gx", "gy", None),
            P("shot", "gx", "gy", None),
            P("shot", "gx", "gy", None),
            P("shot"),
            P("shot", None),
            P("shot", None),
            P("shot", None, None),
            P("shot", None),
            P(),
        ),
        out_specs=(
            P("shot", "gx", "gy", None),
            P("shot", "gx", "gy", None),
            P(("gx", "gy"), "shot", None, None, None, None),
        ),
        check_vma=False,
    )
```

```python
import jax
import jax.numpy as jnp
from jax import lax
from jax.experimental import pallas as pl
from jax.experimental.pallas import tpu as pltpu
from jax.sharding import PartitionSpec as P

MESH = pl.DeviceIdType.MESH
OFFS = 16
STEPS = 3
HALF = 8
NEAR = 4.0 / 3.0
FAR = -1.0 / 12.0
CENTRE = 3.0 * -2.5

CX, CY, NZ = 32, 32, 128
N_GX, N_GY, N_SHOT = 8, 4, 8
TILES = N_GX * N_GY
GROUPS = 16
LAG_B, LAG_C = 3, 5
SG = TILES // GROUPS
CHIPS = N_SHOT // 2
UN = 7
EDGE = 2
EXT = CX + 2 * HALF
BAND = 8
F32 = jnp.float32


def main_kernel(
    vel, s_prev, s_cur, r_prev, r_cur, pos_in, data_in, ap_in, owner_in, amp_in, spos,
    s_out, r_out, g_out,
    w0, w1, w2, w3, bands, old, speed, drive, ysend, yrecv, part, half, final, masks, strip_v, strip,
    pos_ref, data_ref, ap_ref, owner_ref, amp,
    load_sem, xs_sem, xr_sem, ys_sem, yr_sem, ms_sem, mr_sem, es_sem, er_sem, zs_sem, zr_sem,
    bs_sem, br_sem, cs_sem, cr_sem, d_sem, out_sem,
):
    gx, gy, shot = lax.axis_index("gx"), lax.axis_index("gy"), lax.axis_index("shot")
    core = lax.rem(shot, 2)
    chip = lax.div(shot, 2)
    tile = gx * N_GY + gy
    fields = (w0, w1, w2, w3)
    has_left, has_right = gx > 0, gx < N_GX - 1
    has_low, has_high = gy > 0, gy < N_GY - 1

    def pair_a(c):
        return c + 1 - 2 * lax.rem(c, 2)

    def pair_b(c):
        return CHIPS - 1 - c

    def band_a(c):
        return lax.rem(lax.div(c + 1, 2), 2)

    def band_b(c):
        return 2 + lax.div(c, 2)

    chip_a, chip_b = pair_a(chip), pair_b(chip)
    first = jnp.where(core == 0, chip_a, chip_b)
    second = jnp.where(core == 0, chip_b, chip_a)
    band = jnp.where(core == 0, band_a(chip), band_b(chip))
    mate = {"shot": shot + 1 - 2 * core}
    peers = (mate, {"shot": 2 * chip_a}, {"shot": 2 * chip_a + 1}, {"shot": 2 * chip_b}, {"shot": 2 * chip_b + 1})

    barrier = pltpu.get_barrier_semaphore()
    for peer in peers:
        pl.semaphore_signal(barrier, inc=1, device_id=peer, device_id_type=MESH)

    inner = (slice(EDGE, EDGE + CX), slice(8, 8 + CY))
    loads = [
        pltpu.make_async_copy(s_cur.at[0], w0.at[(0,) + inner], load_sem.at[0]),
        pltpu.make_async_copy(r_cur.at[0], w0.at[(1,) + inner], load_sem.at[1]),
        pltpu.make_async_copy(s_prev.at[0], old.at[0], load_sem.at[2]),
        pltpu.make_async_copy(r_prev.at[0], old.at[1], load_sem.at[3]),
        pltpu.make_async_copy(vel, speed, load_sem.at[4]),
    ]
    small = [
        pltpu.make_async_copy(a, b, load_sem.at[6 + i])
        for i, (a, b) in enumerate(
            ((owner_in, owner_ref), (ap_in, ap_ref), (pos_in, pos_ref), (data_in, data_ref), (amp_in, amp))
        )
    ]
    for copy in small + loads:
        copy.start()
    for dz in range(N_GX):
        for dx in range(N_GY):
            if (dz, dx) != (0, 0):
                pl.semaphore_signal(
                    barrier, inc=1, device_id={"gx": lax.rem(gx + dz, N_GX), "gy": lax.rem(gy + dx, N_GY)},
                    device_id_type=MESH,
                )
    for copy in small:
        copy.wait()

    row = owner_ref[pl.ds(tile, 1), :]
    match = row == lax.broadcasted_iota(jnp.int32, (TILES, TILES), 0)
    number = lax.broadcasted_iota(jnp.int32, (TILES, TILES), 1)
    found = jnp.max(jnp.where(match, number, 0), axis=1, keepdims=True)
    strip_v[...] = jnp.broadcast_to(found, (TILES, NZ))
    table = pltpu.make_async_copy(strip_v, strip, load_sem.at[5])
    table.start()
    hit = jnp.max(jnp.where(ap_ref[...] == tile, 1.0, 0.0), axis=1, keepdims=True)
    masks[0] = jnp.broadcast_to(hit, (8, NZ))

    def clear_x(at, wide):
        def body(i, carry):
            for w in fields[:STEPS]:
                for f in range(2):
                    w[f, at + i, 8 : 8 + CY, :] = jnp.zeros((CY, NZ), F32)
            return carry

        lax.fori_loop(0, EDGE, body, 0)

        def body2(i, carry):
            for t in range(STEPS):
                for s in range(4):
                    for f in range(2):
                        bands[t, s, f, wide + i] = jnp.zeros((BAND, NZ), F32)
            return carry

        lax.fori_loop(0, HALF, body2, 0)

    def clear_y(at):
        def body(i, carry):
            for w in fields[:STEPS]:
                for f in range(2):
                    w[f, EDGE + i, at : at + 8, :] = jnp.zeros((8, NZ), F32)
            return carry

        lax.fori_loop(0, CX, body, 0)

    pl.when(jnp.logical_not(has_left))(lambda: clear_x(0, 0))
    pl.when(jnp.logical_not(has_right))(lambda: clear_x(EDGE + CX, HALF + CX))
    pl.when(jnp.logical_not(has_low))(lambda: clear_y(0))
    pl.when(jnp.logical_not(has_high))(lambda: clear_y(8 + CY))

    def inject():
        pos = pos_ref[...]
        rx = lax.shift_right_logical(pos, 14) - gx * CX
        ry = (lax.shift_right_logical(pos, 7) & 127) - gy * CY
        ok = (rx >= 0) & (rx < CX) & (ry >= 0) & (ry < CY)
        cell = jnp.where(ok, rx * CY + ry, -1)
        n = pos.shape[1]
        depth = lax.broadcasted_iota(jnp.int32, (NZ, n), 0) == (pos & 127)
        parts = [[], [], []]
        for t in range(STEPS):
            left = jnp.where(depth, data_ref[t], 0.0)
            for piece in parts:
                cut = left.astype(jnp.bfloat16)
                piece.append(cut)
                left = left - cut.astype(F32)
        parts = [jnp.concatenate(piece, axis=0) for piece in parts]
        rows = 256
        for at in range(0, CX * CY, rows):
            spot = lax.broadcasted_iota(jnp.int32, (rows, n), 0) + at == cell
            spot = jnp.where(spot, 1.0, 0.0).astype(jnp.bfloat16)
            total = None
            for piece in parts:
                term = lax.dot_general(spot, piece, (((1,), (1,)), ((), ())), preferred_element_type=F32)
                total = term if total is None else total + term
            for t in range(STEPS):
                drive[t, at : at + rows, :] = total[:, t * NZ : (t + 1) * NZ]

    inject()

    def x_copy(t, way):
        here, there = ((CX, 0), (EDGE, EDGE + CX))[way]
        return pltpu.make_async_remote_copy(
            src_ref=fields[t].at[:, here : here + EDGE, 8 : 8 + CY, :],
            dst_ref=fields[t].at[:, there : there + EDGE, 8 : 8 + CY, :],
            send_sem=xs_sem.at[t, way], recv_sem=xr_sem.at[t, way],
            device_id={"gx": gx + 1 - 2 * way}, device_id_type=MESH,
        )

    def y_copy(t, way):
        return pltpu.make_async_remote_copy(
            src_ref=ysend.at[t, way], dst_ref=yrecv.at[t, way],
            send_sem=ys_sem.at[t, way], recv_sem=yr_sem.at[t, way],
            device_id={"gy": gy + 1 - 2 * way}, device_id_type=MESH,
        )

    x_to, x_from = (has_right, has_left), (has_left, has_right)
    y_to, y_from = (has_high, has_low), (has_low, has_high)

    def send_x(t):
        for way in range(2):
            pl.when(x_to[way])(lambda: x_copy(t, way).start())

    def got_x(t):
        for way in range(2):
            pl.when(x_from[way])(lambda: x_copy(t, way).wait_recv())

    def y_rows(i, f, j):
        return pl.ds(f * 2 * CX + pl.multiple_of(i * 8, 8) + 2 * j, 2)

    def pack_y(t):
        w = fields[t]

        def body(i, carry):
            for f in range(2):
                for j in range(4):
                    ysend[t, 0, y_rows(i, f, j), :] = w[f, EDGE + i * 4 + j, 6 + CY : 8 + CY, :]
                    ysend[t, 1, y_rows(i, f, j), :] = w[f, EDGE + i * 4 + j, 8:10, :]
            return carry

        lax.fori_loop(0, CX // 4, body, 0, unroll=4)

    def send_y(t):
        for way in range(2):
            pl.when(y_to[way])(lambda: y_copy(t, way).start())

    def got_y(t):
        w = fields[t]
        for way in range(2):
            at = (6, 8 + CY)[way]

            def take(way=way, at=at):
                y_copy(t, way).wait_recv()

                def body(i, carry):
                    for f in range(2):
                        for j in range(4):
                            w[f, EDGE + i * 4 + j, at : at + 2, :] = yrecv[t, way, y_rows(i, f, j), :]
                    return carry

                lax.fori_loop(0, CX // 4, body, 0, unroll=4)

            pl.when(y_from[way])(take)

    targets = (
        (mate, 1, jnp.where(core == 0, band_b(chip), band_a(chip))),
        ({"shot": 2 * chip_a}, 2 + core, band_a(chip_a)),
        ({"shot": 2 * chip_b + 1}, 2 + core, band_b(chip_b)),
    )
    cuts = ((0, 8), (CX - 8, 8), (8, CX - 16))

    def m_copy(target):
        to, slot, _ = targets[target]
        return pltpu.make_async_remote_copy(
            src_ref=masks.at[0], dst_ref=masks.at[slot],
            send_sem=ms_sem.at[target], recv_sem=mr_sem.at[slot - 1],
            device_id=to, device_id_type=MESH,
        )

    def m_arrival(slot):
        return pltpu.make_async_copy(masks.at[slot], masks.at[slot], mr_sem.at[slot - 1])

    def band_rows(b):
        return pl.ds(pl.multiple_of(8 + BAND * b, 8), BAND)

    def e_copy(t, target, cut):
        to, slot, b = targets[target]
        at, n = cuts[cut]
        return pltpu.make_async_remote_copy(
            src_ref=fields[t].at[:, EDGE + at : EDGE + at + n, band_rows(b), :],
            dst_ref=bands.at[t - 1, slot, :, HALF + at : HALF + at + n],
            send_sem=es_sem.at[t - 1, target, cut], recv_sem=er_sem.at[t - 1, slot - 1, cut],
            device_id=to, device_id_type=MESH,
        )

    def e_arrival(t, slot, cut):
        at, n = cuts[cut]
        ref = bands.at[t - 1, slot, :, HALF + at : HALF + at + n]
        return pltpu.make_async_copy(ref, ref, er_sem.at[t - 1, slot - 1, cut])

    def e_own(t):
        return pltpu.make_async_copy(
            fields[t].at[:, EDGE : EDGE + CX, band_rows(band), :],
            bands.at[t - 1, 0, :, HALF : HALF + CX],
            es_sem.at[t - 1, 3, 0],
        )

    def send_e(t):
        e_own(t).start()
        for cut in range(3):
            for target in (1, 2, 0):
                e_copy(t, target, cut).start()

    def z_copy(t, way, f):
        here, there, n = (
            ((CX + 1, 1, HALF - 1), (CX, 0, HALF)),
            ((HALF, HALF + CX, HALF), (HALF, HALF + CX, HALF - 1)),
        )[way][f]
        return pltpu.make_async_remote_copy(
            src_ref=bands.at[t - 1, :, f, here : here + n],
            dst_ref=bands.at[t - 1, :, f, there : there + n],
            send_sem=zs_sem.at[t - 1, way, f], recv_sem=zr_sem.at[t - 1, way, f],
            device_id={"gx": gx + 1 - 2 * way}, device_id_type=MESH,
        )

    def send_z(t):
        e_own(t).wait()
        for slot in range(1, 4):
            for cut in range(2):
                e_arrival(t, slot, cut).wait()
        for way in range(2):
            for f in range(2):
                pl.when(x_to[way])(lambda: z_copy(t, way, f).start())

    lane = lax.broadcasted_iota(jnp.int32, (8, NZ), 1)
    near_up = jnp.where(lane < NZ - 1, NEAR, 0.0)
    near_down = jnp.where(lane > 0, NEAR, 0.0)
    far_up = jnp.where(lane < NZ - 2, FAR, 0.0)
    far_down = jnp.where(lane > 1, FAR, 0.0)
    spot = lax.broadcasted_iota(jnp.int32, (8, NZ), 0) * NZ + lane
    p = spos[0]
    lx = lax.shift_right_logical(p, 14) - gx * CX
    ly = (lax.shift_right_logical(p, 7) & 127) - gy * CY
    within = (lx >= 0) & (lx < CX) & (ly >= 0) & (ly < CY)
    where = jnp.where(within, (lx * CY + ly) * NZ + (p & 127), -1)

    def cells(t, x, ys):
        w, new = fields[t], fields[t + 1]
        X = x + EDGE
        for y in ys:
            Y = 8 + 8 * y
            v = speed[x, 8 * y : 8 * y + 8, :]
            for f in range(2):
                c = w[f, X, Y : Y + 8, :]
                near = (w[f, X + 1, Y : Y + 8, :] + w[f, X - 1, Y : Y + 8, :]) + (
                    w[f, X, Y + 1 : Y + 9, :] + w[f, X, Y - 1 : Y + 7, :]
                )
                far = (w[f, X + 2, Y : Y + 8, :] + w[f, X - 2, Y : Y + 8, :]) + (
                    w[f, X, Y + 2 : Y + 10, :] + w[f, X, Y - 2 : Y + 6, :]
                )
                lap = CENTRE * c + NEAR * near + FAR * far
                lap = lap + (near_up * pltpu.roll(c, NZ - 1, 1) + near_down * pltpu.roll(c, 1, 1))
                lap = lap + (far_up * pltpu.roll(c, NZ - 2, 1) + far_down * pltpu.roll(c, 2, 1))
                if t == 0:
                    before = old[f, x, 8 * y : 8 * y + 8, :]
                else:
                    before = fields[t - 1][f, X, Y : Y + 8, :]
                value = (2.0 * c - before) + v * lap
                if f == 0:
                    add = jnp.where(spot == where - (x * CY + 8 * y) * NZ, amp[0, t], 0.0)
                else:
                    add = drive[t, pl.ds(pl.multiple_of(x * CY + 8 * y, 8), 8), :]
                new[f, X, Y : Y + 8, :] = value + add

    def inside_cells(t):
        def body(i, carry):
            for j in range(UN):
                cells(t, EDGE + UN * i + j, (1, 2))
            return carry

        lax.fori_loop(0, (CX - 2 * EDGE) // UN, body, 0)

    def rim_cells(t):
        def body(i, carry):
            for j in range(UN):
                cells(t, EDGE + UN * i + j, (0, 3))
            return carry

        def ends(i, carry):
            cells(t, i + jnp.where(i >= EDGE, CX - 2 * EDGE, 0), (0, 1, 2, 3))
            return carry

        lax.fori_loop(0, 2 * EDGE, ends, 0)
        lax.fori_loop(0, (CX - 2 * EDGE) // UN, body, 0)

    for copy in loads[:2]:
        copy.wait()
    pack_y(0)
    pl.semaphore_wait(barrier, TILES - 1 + len(peers))
    send_x(0)
    send_y(0)
    for target in range(3):
        m_copy(target).start()
    for copy in loads[2:]:
        copy.wait()
    table.wait()
    for t in range(STEPS):
        inside_cells(t)
        got_x(t)
        got_y(t)
        rim_cells(t)
        if t + 1 < STEPS:
            send_x(t + 1)
            pack_y(t + 1)
            send_y(t + 1)
        send_e(t + 1)
        if t:
            send_z(t)
    stores = [
        pltpu.make_async_copy(w3.at[(f,) + inner], (s_out, r_out)[f].at[0], out_sem.at[f]) for f in range(2)
    ]
    for copy in stores:
        copy.start()
    send_z(STEPS)
    for slot in range(1, 4):
        m_arrival(slot).wait()
    for t in range(1, STEPS + 1):
        for slot in range(1, 4):
            e_arrival(t, slot, 2).wait()
    for t in range(1, STEPS + 1):
        for way in range(2):
            for f in range(2):
                pl.when(x_from[way])(lambda: z_copy(t, way, f).wait_recv())

    dxs = (2, 1, 3, 0)
    dzs = ((3, 5), (4, 2), (6, 1), (7, 0))

    def to_whom(group, i):
        dx = jnp.int32(dxs[0])
        for g in range(1, N_GY):
            dx = jnp.where(lax.div(group, N_GX // SG) == g, dxs[g], dx)
        dz = jnp.int32(dzs[0][0])
        for g in range(N_GX // SG):
            for j in range(SG):
                dz = jnp.where((lax.rem(group, N_GX // SG) == g) & (i == j), dzs[g][j], dz)
        return lax.rem(gx + dz, N_GX), lax.rem(gy + dx, N_GY)

    place = []
    for c in range(CHIPS):
        at = jnp.where(c == chip, 0, jnp.where(c == first, 1, jnp.where(c == second, 2, 3)))
        place.append(at)

    def correlate(group):
        def body(i, carry):
            ox, oy = to_whom(group, i)
            k = jnp.clip(strip[ox * N_GY + oy, 0], 0, CX - 1)
            m = [masks[s] for s in range(4)]
            for h in range(OFFS):
                total = None
                for s in range(4):
                    one = None
                    for t in range(STEPS):
                        term = bands[t, s, 0, k + OFFS - h] * bands[t, s, 1, k + h]
                        one = term if one is None else one + term
                    one = one * m[s]
                    total = one if total is None else total + one
                part[group, place[h // 4], i, h % 4] = total
            return carry

        lax.fori_loop(0, SG, body, 0)

    def b_copy(group):
        return pltpu.make_async_remote_copy(
            src_ref=part.at[group, 2:4], dst_ref=half.at[group],
            send_sem=bs_sem.at[group], recv_sem=br_sem.at[group],
            device_id={"shot": 2 * second + core}, device_id_type=MESH,
        )

    def strips(group):
        return pl.ds(group * SG, SG)

    def out_rows(b):
        return pl.ds(pl.multiple_of(BAND * b, 8), BAND)

    homes = ((mate, 0, 0, 2 * (1 - core)), ({"shot": 2 * first}, 1 + core, 1, 0), ({"shot": 2 * first + 1}, 1 + core, 1, 2))

    def c_copy(group, home):
        to, slot, at, h = homes[home]
        return pltpu.make_async_remote_copy(
            src_ref=part.at[group, at, :, pl.ds(h, 2)],
            dst_ref=final.at[strips(group), :, out_rows(band), :],
            send_sem=cs_sem.at[group, home], recv_sem=cr_sem.at[group, slot],
            device_id=to, device_id_type=MESH,
        )

    sources = (targets[0][2], band_a(chip_a), band_b(chip_b))

    def c_arrival(group, slot):
        ref = final.at[strips(group), :, out_rows(sources[slot]), :]
        return pltpu.make_async_copy(ref, ref, cr_sem.at[group, slot])

    def d_copy(group, i):
        ox, oy = to_whom(group, i)
        return pltpu.make_async_remote_copy(
            src_ref=final.at[group * SG + i], dst_ref=g_out.at[0, :, tile, 0],
            send_sem=d_sem.at[0], recv_sem=d_sem.at[1],
            device_id={"gx": ox, "gy": oy}, device_id_type=MESH,
        )

    def own_copy():
        return pltpu.make_async_copy(final.at[TILES - 1], g_out.at[0, :, tile, 0], d_sem.at[2])

    def from_second(group):
        b_copy(group).wait_recv()

        def body(i, carry):
            for at in (1, 0):
                part[group, at, i] = part[group, at, i] + half[group, at, i]
            return carry

        lax.fori_loop(0, SG, body, 0)
        for home in (1, 2, 0):
            c_copy(group, home).start()

        def keep(i, carry):
            final[group * SG + i, :, out_rows(band), :] = part[group, 0, i, pl.ds(2 * core, 2)]
            return carry

        lax.fori_loop(0, SG, keep, 0)

    def from_first(group):
        for slot in range(3):
            c_arrival(group, slot).wait()

        def body(i, carry):
            mine = (group == GROUPS - 1) & (i == SG - 1)

            @pl.when(mine)
            def _():
                own_copy().start()

            @pl.when(jnp.logical_not(mine))
            def _():
                d_copy(group, i).start()

            return carry

        lax.fori_loop(0, SG, body, 0)

    def stage(it, carry):
        @pl.when(it < GROUPS)
        def _():
            correlate(it)
            b_copy(it).start()

        @pl.when((it >= LAG_B) & (it < GROUPS + LAG_B))
        def _():
            from_second(it - LAG_B)

        @pl.when(it >= LAG_C)
        def _():
            from_first(it - LAG_C)

        return carry

    lax.fori_loop(0, GROUPS + LAG_C, stage, 0)

    for t in range(STEPS):
        for way in range(2):
            pl.when(x_to[way])(lambda: x_copy(t, way).wait_send())
            pl.when(y_to[way])(lambda: y_copy(t, way).wait_send())
            for f in range(2):
                pl.when(x_to[way])(lambda: z_copy(t + 1, way, f).wait_send())
        for target in range(3):
            for cut in range(3):
                e_copy(t + 1, target, cut).wait_send()
    for target in range(3):
        m_copy(target).wait_send()

    def drain(group, carry):
        b_copy(group).wait_send()
        for home in range(3):
            c_copy(group, home).wait_send()
        return carry

    lax.fori_loop(0, GROUPS, drain, 0)
    for copy in stores:
        copy.wait()
    own_copy().wait()
    sent = final.at[0 : TILES - 1]
    pltpu.make_async_copy(sent, sent, d_sem.at[0]).wait()
    arrived = g_out.at[0, :, 0 : TILES - 1, 0]
    pltpu.make_async_copy(arrived, arrived, d_sem.at[1]).wait()


def hand_over_kernel(a, b, c, x, y, z, sem):
    copies = [pltpu.make_async_copy(v, w, sem.at[i]) for i, (v, w) in enumerate(((a, x), (b, y), (c, z)))]
    for copy in copies:
        copy.start()
    for copy in copies:
        copy.wait()


def body(vel_coef, src_prev, src_cur, rcv_prev, rcv_cur, src_pos, src_amp, rcv_pos, rcv_data, aperture, owner):
    big = [
        pltpu.with_memory_space_constraint(v, pltpu.HBM)
        for v in (
            vel_coef, src_prev, src_cur, rcv_prev, rcv_cur,
            rcv_pos, jnp.transpose(rcv_data, (1, 0, 2)), aperture, owner, src_amp,
        )
    ]
    whole = pl.BlockSpec(memory_space=pl.ANY)
    DMA = pltpu.SemaphoreType.DMA
    wave = pltpu.VMEM((2, CX + 2 * EDGE, CY + 16, NZ), F32)
    done = pl.pallas_call(
        main_kernel,
        out_shape=(
            jax.ShapeDtypeStruct(src_cur.shape, F32),
            jax.ShapeDtypeStruct(rcv_cur.shape, F32),
            jax.ShapeDtypeStruct((1, 2, TILES, 1, CY, NZ), F32),
        ),
        in_specs=[pl.BlockSpec(memory_space=pltpu.HBM)] * 10 + [pl.BlockSpec(memory_space=pltpu.SMEM)],
        out_specs=(whole, whole, whole),
        scratch_shapes=[
            wave, wave, wave, wave,
            pltpu.VMEM((STEPS, 4, 2, EXT, BAND, NZ), F32),
            pltpu.VMEM((2, CX, CY, NZ), F32),
            pltpu.VMEM((CX, CY, NZ), F32),
            pltpu.VMEM((STEPS, CX * CY, NZ), F32),
            pltpu.VMEM((STEPS, 2, 4 * CX, NZ), F32),
            pltpu.VMEM((STEPS, 2, 4 * CX, NZ), F32),
            pltpu.VMEM((GROUPS, CHIPS, SG, 4, BAND, NZ), F32),
            pltpu.VMEM((GROUPS, 2, SG, 4, BAND, NZ), F32),
            pltpu.VMEM((TILES, 2, CY, NZ), F32),
            pltpu.VMEM((4, 8, NZ), F32),
            pltpu.VMEM((TILES, NZ), jnp.int32),
            pltpu.SMEM((TILES, NZ), jnp.int32),
            pltpu.VMEM(rcv_pos.shape, jnp.int32),
            pltpu.VMEM((STEPS, 1, rcv_pos.shape[1]), F32),
            pltpu.VMEM(aperture.shape, jnp.int32),
            pltpu.VMEM(owner.shape, jnp.int32),
            pltpu.SMEM(src_amp.shape, F32),
            DMA((12,)),
            DMA((STEPS, 2)), DMA((STEPS, 2)), DMA((STEPS, 2)), DMA((STEPS, 2)),
            DMA((3,)), DMA((3,)),
            DMA((STEPS, 4, 3)), DMA((STEPS, 3, 3)),
            DMA((STEPS, 2, 2)), DMA((STEPS, 2, 2)),
            DMA((GROUPS,)), DMA((GROUPS,)),
            DMA((GROUPS, 3)), DMA((GROUPS, 3)),
            DMA((3,)), DMA((2,)),
        ],
        compiler_params=pltpu.CompilerParams(
            collective_id=0, has_side_effects=True, vmem_limit_bytes=48 * 1024 * 1024
        ),
        name="migrate",
    )(*big, src_pos)
    return pl.pallas_call(
        hand_over_kernel,
        out_shape=tuple(jax.ShapeDtypeStruct(v.shape, v.dtype) for v in done),
        in_specs=[whole] * 3,
        out_specs=(whole,) * 3,
        scratch_shapes=[DMA((3,))],
        compiler_params=pltpu.CompilerParams(vmem_limit_bytes=1024 * 1024),
        name="hand_over",
    )(*done)


def solution(mesh):
    return jax.shard_map(
        body,
        mesh=mesh,
        in_specs=(
            P("gx", "gy", None),
            P("shot", "gx", "gy", None),
            P("shot", "gx", "gy", None),
            P("shot", "gx", "gy", None),
            P("shot", "gx", "gy", None),
            P("shot"),
            P("shot", None),
            P("shot", None),
            P("shot", None, None),
            P("shot", None),
            P(),
        ),
        out_specs=(
            P("shot", "gx", "gy", None),
            P("shot", "gx", "gy", None),
            P(("gx", "gy"), "shot", None, None, None, None),
        ),
        check_vma=False,
    )
```

```python
import jax
import jax.numpy as jnp
from jax import lax
from jax.experimental import pallas as pl
from jax.experimental.pallas import tpu as pltpu
from jax.sharding import PartitionSpec as P

MESH = pl.DeviceIdType.MESH
OFFS = 16
STEPS = 3
HALF = 8
NEAR = 4.0 / 3.0
FAR = -1.0 / 12.0
CENTRE = 3.0 * -2.5

CX, CY, NZ = 32, 32, 128
N_GX, N_GY, N_SHOT = 8, 4, 8
TILES = N_GX * N_GY
GROUPS = 16
LAG_B, LAG_C = 3, 5
SG = TILES // GROUPS
CHIPS = N_SHOT // 2
UN = 7
EDGE = 2
EXT = CX + 2 * HALF
BAND = 8
F32 = jnp.float32


def main_kernel(
    vel, s_prev, s_cur, r_prev, r_cur, pos_in, data_in, ap_in, owner_in, amp_in, spos,
    s_out, r_out, g_out,
    w0, w1, w2, w3, bands, old, speed, drive, ysend, yrecv, part, half, final, masks, strip_v, strip,
    pos_ref, data_ref, ap_ref, owner_ref, amp,
    load_sem, xs_sem, xr_sem, ys_sem, yr_sem, ms_sem, mr_sem, es_sem, er_sem, zs_sem, zr_sem,
    bs_sem, br_sem, cs_sem, cr_sem, d_sem, out_sem,
):
    gx, gy, shot = lax.axis_index("gx"), lax.axis_index("gy"), lax.axis_index("shot")
    core = lax.rem(shot, 2)
    chip = lax.div(shot, 2)
    tile = gx * N_GY + gy
    fields = (w0, w1, w2, w3)
    has_left, has_right = gx > 0, gx < N_GX - 1
    has_low, has_high = gy > 0, gy < N_GY - 1

    def pair_a(c):
        return c + 1 - 2 * lax.rem(c, 2)

    def pair_b(c):
        return CHIPS - 1 - c

    def band_a(c):
        return lax.rem(lax.div(c + 1, 2), 2)

    def band_b(c):
        return 2 + lax.div(c, 2)

    chip_a, chip_b = pair_a(chip), pair_b(chip)
    first = jnp.where(core == 0, chip_a, chip_b)
    second = jnp.where(core == 0, chip_b, chip_a)
    band = jnp.where(core == 0, band_a(chip), band_b(chip))
    mate = {"shot": shot + 1 - 2 * core}
    peers = (mate, {"shot": 2 * chip_a}, {"shot": 2 * chip_a + 1}, {"shot": 2 * chip_b}, {"shot": 2 * chip_b + 1})

    barrier = pltpu.get_barrier_semaphore()
    for peer in peers:
        pl.semaphore_signal(barrier, inc=1, device_id=peer, device_id_type=MESH)

    inner = (slice(EDGE, EDGE + CX), slice(8, 8 + CY))
    loads = [
        pltpu.make_async_copy(s_cur.at[0], w0.at[(0,) + inner], load_sem.at[0]),
        pltpu.make_async_copy(r_cur.at[0], w0.at[(1,) + inner], load_sem.at[1]),
        pltpu.make_async_copy(s_prev.at[0], old.at[0], load_sem.at[2]),
        pltpu.make_async_copy(r_prev.at[0], old.at[1], load_sem.at[3]),
        pltpu.make_async_copy(vel, speed, load_sem.at[4]),
    ]
    small = [
        pltpu.make_async_copy(a, b, load_sem.at[6 + i])
        for i, (a, b) in enumerate(
            ((owner_in, owner_ref), (ap_in, ap_ref), (pos_in, pos_ref), (data_in, data_ref), (amp_in, amp))
        )
    ]
    for copy in small + loads:
        copy.start()
    for dz in range(N_GX):
        for dx in range(N_GY):
            if (dz, dx) != (0, 0):
                pl.semaphore_signal(
                    barrier, inc=1, device_id={"gx": lax.rem(gx + dz, N_GX), "gy": lax.rem(gy + dx, N_GY)},
                    device_id_type=MESH,
                )
    for copy in small:
        copy.wait()

    row = owner_ref[pl.ds(tile, 1), :]
    match = row == lax.broadcasted_iota(jnp.int32, (TILES, TILES), 0)
    number = lax.broadcasted_iota(jnp.int32, (TILES, TILES), 1)
    found = jnp.max(jnp.where(match, number, 0), axis=1, keepdims=True)
    strip_v[...] = jnp.broadcast_to(found, (TILES, NZ))
    table = pltpu.make_async_copy(strip_v, strip, load_sem.at[5])
    table.start()
    hit = jnp.max(jnp.where(ap_ref[...] == tile, 1.0, 0.0), axis=1, keepdims=True)
    masks[0] = jnp.broadcast_to(hit, (8, NZ))

    def clear_x(at, wide):
        def body(i, carry):
            for w in fields[:STEPS]:
                for f in range(2):
                    w[f, at + i, 8 : 8 + CY, :] = jnp.zeros((CY, NZ), F32)
            return carry

        lax.fori_loop(0, EDGE, body, 0)

        def body2(i, carry):
            for t in range(STEPS):
                for s in range(4):
                    for f in range(2):
                        bands[t, s, f, wide + i] = jnp.zeros((BAND, NZ), F32)
            return carry

        lax.fori_loop(0, HALF, body2, 0)

    def clear_y(at):
        def body(i, carry):
            for w in fields[:STEPS]:
                for f in range(2):
                    w[f, EDGE + i, at : at + 8, :] = jnp.zeros((8, NZ), F32)
            return carry

        lax.fori_loop(0, CX, body, 0)

    pl.when(jnp.logical_not(has_left))(lambda: clear_x(0, 0))
    pl.when(jnp.logical_not(has_right))(lambda: clear_x(EDGE + CX, HALF + CX))
    pl.when(jnp.logical_not(has_low))(lambda: clear_y(0))
    pl.when(jnp.logical_not(has_high))(lambda: clear_y(8 + CY))

    def inject():
        pos = pos_ref[...]
        rx = lax.shift_right_logical(pos, 14) - gx * CX
        ry = (lax.shift_right_logical(pos, 7) & 127) - gy * CY
        ok = (rx >= 0) & (rx < CX) & (ry >= 0) & (ry < CY)
        cell = jnp.where(ok, rx * CY + ry, -1)
        n = pos.shape[1]
        depth = lax.broadcasted_iota(jnp.int32, (NZ, n), 0) == (pos & 127)
        parts = [[], [], []]
        for t in range(STEPS):
            left = jnp.where(depth, data_ref[t], 0.0)
            for piece in parts:
                cut = left.astype(jnp.bfloat16)
                piece.append(cut)
                left = left - cut.astype(F32)
        parts = [jnp.concatenate(piece, axis=0) for piece in parts]
        rows = 256
        for at in range(0, CX * CY, rows):
            spot = lax.broadcasted_iota(jnp.int32, (rows, n), 0) + at == cell
            spot = jnp.where(spot, 1.0, 0.0).astype(jnp.bfloat16)
            total = None
            for piece in parts:
                term = lax.dot_general(spot, piece, (((1,), (1,)), ((), ())), preferred_element_type=F32)
                total = term if total is None else total + term
            for t in range(STEPS):
                drive[t, at : at + rows, :] = total[:, t * NZ : (t + 1) * NZ]

    inject()

    def x_copy(t, way):
        here, there = ((CX, 0), (EDGE, EDGE + CX))[way]
        return pltpu.make_async_remote_copy(
            src_ref=fields[t].at[:, here : here + EDGE, 8 : 8 + CY, :],
            dst_ref=fields[t].at[:, there : there + EDGE, 8 : 8 + CY, :],
            send_sem=xs_sem.at[t, way], recv_sem=xr_sem.at[t, way],
            device_id={"gx": gx + 1 - 2 * way}, device_id_type=MESH,
        )

    def y_copy(t, way):
        return pltpu.make_async_remote_copy(
            src_ref=ysend.at[t, way], dst_ref=yrecv.at[t, way],
            send_sem=ys_sem.at[t, way], recv_sem=yr_sem.at[t, way],
            device_id={"gy": gy + 1 - 2 * way}, device_id_type=MESH,
        )

    x_to, x_from = (has_right, has_left), (has_left, has_right)
    y_to, y_from = (has_high, has_low), (has_low, has_high)

    def send_x(t):
        for way in range(2):
            pl.when(x_to[way])(lambda: x_copy(t, way).start())

    def got_x(t):
        for way in range(2):
            pl.when(x_from[way])(lambda: x_copy(t, way).wait_recv())

    def y_rows(i, f, j):
        return pl.ds(f * 2 * CX + pl.multiple_of(i * 8, 8) + 2 * j, 2)

    def pack_y(t):
        w = fields[t]

        def body(i, carry):
            for f in range(2):
                for j in range(4):
                    ysend[t, 0, y_rows(i, f, j), :] = w[f, EDGE + i * 4 + j, 6 + CY : 8 + CY, :]
                    ysend[t, 1, y_rows(i, f, j), :] = w[f, EDGE + i * 4 + j, 8:10, :]
            return carry

        lax.fori_loop(0, CX // 4, body, 0, unroll=4)

    def send_y(t):
        for way in range(2):
            pl.when(y_to[way])(lambda: y_copy(t, way).start())

    def got_y(t):
        w = fields[t]
        for way in range(2):
            at = (6, 8 + CY)[way]

            def take(way=way, at=at):
                y_copy(t, way).wait_recv()

                def body(i, carry):
                    for f in range(2):
                        for j in range(4):
                            w[f, EDGE + i * 4 + j, at : at + 2, :] = yrecv[t, way, y_rows(i, f, j), :]
                    return carry

                lax.fori_loop(0, CX // 4, body, 0, unroll=4)

            pl.when(y_from[way])(take)

    targets = (
        (mate, 1, jnp.where(core == 0, band_b(chip), band_a(chip))),
        ({"shot": 2 * chip_a}, 2 + core, band_a(chip_a)),
        ({"shot": 2 * chip_b + 1}, 2 + core, band_b(chip_b)),
    )
    cuts = ((0, 8), (CX - 8, 8), (8, CX - 16))

    def m_copy(target):
        to, slot, _ = targets[target]
        return pltpu.make_async_remote_copy(
            src_ref=masks.at[0], dst_ref=masks.at[slot],
            send_sem=ms_sem.at[target], recv_sem=mr_sem.at[slot - 1],
            device_id=to, device_id_type=MESH,
        )

    def m_arrival(slot):
        return pltpu.make_async_copy(masks.at[slot], masks.at[slot], mr_sem.at[slot - 1])

    def band_rows(b):
        return pl.ds(pl.multiple_of(8 + BAND * b, 8), BAND)

    def e_copy(t, target, cut):
        to, slot, b = targets[target]
        at, n = cuts[cut]
        return pltpu.make_async_remote_copy(
            src_ref=fields[t].at[:, EDGE + at : EDGE + at + n, band_rows(b), :],
            dst_ref=bands.at[t - 1, slot, :, HALF + at : HALF + at + n],
            send_sem=es_sem.at[t - 1, target, cut], recv_sem=er_sem.at[t - 1, slot - 1, cut],
            device_id=to, device_id_type=MESH,
        )

    def e_arrival(t, slot, cut):
        at, n = cuts[cut]
        ref = bands.at[t - 1, slot, :, HALF + at : HALF + at + n]
        return pltpu.make_async_copy(ref, ref, er_sem.at[t - 1, slot - 1, cut])

    def e_own(t):
        return pltpu.make_async_copy(
            fields[t].at[:, EDGE : EDGE + CX, band_rows(band), :],
            bands.at[t - 1, 0, :, HALF : HALF + CX],
            es_sem.at[t - 1, 3, 0],
        )

    def send_e(t):
        e_own(t).start()
        for cut in range(3):
            for target in (1, 2, 0):
                e_copy(t, target, cut).start()

    def z_copy(t, way, f):
        here, there, n = (
            ((CX + 1, 1, HALF - 1), (CX, 0, HALF)),
            ((HALF, HALF + CX, HALF), (HALF, HALF + CX, HALF - 1)),
        )[way][f]
        return pltpu.make_async_remote_copy(
            src_ref=bands.at[t - 1, :, f, here : here + n],
            dst_ref=bands.at[t - 1, :, f, there : there + n],
            send_sem=zs_sem.at[t - 1, way, f], recv_sem=zr_sem.at[t - 1, way, f],
            device_id={"gx": gx + 1 - 2 * way}, device_id_type=MESH,
        )

    def send_z(t):
        e_own(t).wait()
        for slot in range(1, 4):
            for cut in range(2):
                e_arrival(t, slot, cut).wait()
        for way in range(2):
            for f in range(2):
                pl.when(x_to[way])(lambda: z_copy(t, way, f).start())

    lane = lax.broadcasted_iota(jnp.int32, (8, NZ), 1)
    near_up = jnp.where(lane < NZ - 1, NEAR, 0.0)
    near_down = jnp.where(lane > 0, NEAR, 0.0)
    far_up = jnp.where(lane < NZ - 2, FAR, 0.0)
    far_down = jnp.where(lane > 1, FAR, 0.0)
    spot = lax.broadcasted_iota(jnp.int32, (8, NZ), 0) * NZ + lane
    p = spos[0]
    lx = lax.shift_right_logical(p, 14) - gx * CX
    ly = (lax.shift_right_logical(p, 7) & 127) - gy * CY
    within = (lx >= 0) & (lx < CX) & (ly >= 0) & (ly < CY)
    where = jnp.where(within, (lx * CY + ly) * NZ + (p & 127), -1)

    def cells(t, x, ys):
        w, new = fields[t], fields[t + 1]
        X = x + EDGE
        for y in ys:
            Y = 8 + 8 * y
            v = speed[x, 8 * y : 8 * y + 8, :]
            for f in range(2):
                c = w[f, X, Y : Y + 8, :]
                near = (w[f, X + 1, Y : Y + 8, :] + w[f, X - 1, Y : Y + 8, :]) + (
                    w[f, X, Y + 1 : Y + 9, :] + w[f, X, Y - 1 : Y + 7, :]
                )
                far = (w[f, X + 2, Y : Y + 8, :] + w[f, X - 2, Y : Y + 8, :]) + (
                    w[f, X, Y + 2 : Y + 10, :] + w[f, X, Y - 2 : Y + 6, :]
                )
                lap = CENTRE * c + NEAR * near + FAR * far
                lap = lap + (near_up * pltpu.roll(c, NZ - 1, 1) + near_down * pltpu.roll(c, 1, 1))
                lap = lap + (far_up * pltpu.roll(c, NZ - 2, 1) + far_down * pltpu.roll(c, 2, 1))
                if t == 0:
                    before = old[f, x, 8 * y : 8 * y + 8, :]
                else:
                    before = fields[t - 1][f, X, Y : Y + 8, :]
                value = (2.0 * c - before) + v * lap
                if f == 0:
                    add = jnp.where(spot == where - (x * CY + 8 * y) * NZ, amp[0, t], 0.0)
                else:
                    add = drive[t, pl.ds(pl.multiple_of(x * CY + 8 * y, 8), 8), :]
                new[f, X, Y : Y + 8, :] = value + add

    def inside_cells(t):
        def body(i, carry):
            for j in range(UN):
                cells(t, EDGE + UN * i + j, (1, 2))
            return carry

        lax.fori_loop(0, (CX - 2 * EDGE) // UN, body, 0)

    def rim_cells(t):
        def body(i, carry):
            for j in range(UN):
                cells(t, EDGE + UN * i + j, (0, 3))
            return carry

        def ends(i, carry):
            cells(t, i + jnp.where(i >= EDGE, CX - 2 * EDGE, 0), (0, 1, 2, 3))
            return carry

        lax.fori_loop(0, 2 * EDGE, ends, 0)
        if t + 1 < STEPS:
            send_x(t + 1)
        lax.fori_loop(0, (CX - 2 * EDGE) // UN, body, 0)

    for copy in loads[:2]:
        copy.wait()
    pack_y(0)
    pl.semaphore_wait(barrier, TILES - 1 + len(peers))
    send_x(0)
    send_y(0)
    for target in range(3):
        m_copy(target).start()
    for copy in loads[2:]:
        copy.wait()
    table.wait()
    for t in range(STEPS):
        inside_cells(t)
        got_x(t)
        got_y(t)
        rim_cells(t)
        if t + 1 < STEPS:
            pack_y(t + 1)
            send_y(t + 1)
        send_e(t + 1)
        if t:
            send_z(t)
    stores = [
        pltpu.make_async_copy(w3.at[(f,) + inner], (s_out, r_out)[f].at[0], out_sem.at[f]) for f in range(2)
    ]
    for copy in stores:
        copy.start()
    send_z(STEPS)
    for slot in range(1, 4):
        m_arrival(slot).wait()
    for t in range(1, STEPS + 1):
        for slot in range(1, 4):
            e_arrival(t, slot, 2).wait()
    for t in range(1, STEPS + 1):
        for way in range(2):
            for f in range(2):
                pl.when(x_from[way])(lambda: z_copy(t, way, f).wait_recv())

    dxs = (2, 1, 3, 0)
    dzs = ((3, 5), (4, 2), (6, 1), (7, 0))

    def to_whom(group, i):
        dx = jnp.int32(dxs[0])
        for g in range(1, N_GY):
            dx = jnp.where(lax.div(group, N_GX // SG) == g, dxs[g], dx)
        dz = jnp.int32(dzs[0][0])
        for g in range(N_GX // SG):
            for j in range(SG):
                dz = jnp.where((lax.rem(group, N_GX // SG) == g) & (i == j), dzs[g][j], dz)
        return lax.rem(gx + dz, N_GX), lax.rem(gy + dx, N_GY)

    place = []
    for c in range(CHIPS):
        at = jnp.where(c == chip, 0, jnp.where(c == first, 1, jnp.where(c == second, 2, 3)))
        place.append(at)

    def correlate(group):
        def body(i, carry):
            ox, oy = to_whom(group, i)
            k = jnp.clip(strip[ox * N_GY + oy, 0], 0, CX - 1)
            m = [masks[s] for s in range(4)]
            for h in range(OFFS):
                total = None
                for s in range(4):
                    one = None
                    for t in range(STEPS):
                        term = bands[t, s, 0, k + OFFS - h] * bands[t, s, 1, k + h]
                        one = term if one is None else one + term
                    one = one * m[s]
                    total = one if total is None else total + one
                part[group, place[h // 4], i, h % 4] = total
            return carry

        lax.fori_loop(0, SG, body, 0)

    def b_copy(group):
        return pltpu.make_async_remote_copy(
            src_ref=part.at[group, 2:4], dst_ref=half.at[group],
            send_sem=bs_sem.at[group], recv_sem=br_sem.at[group],
            device_id={"shot": 2 * second + core}, device_id_type=MESH,
        )

    def strips(group):
        return pl.ds(group * SG, SG)

    def out_rows(b):
        return pl.ds(pl.multiple_of(BAND * b, 8), BAND)

    homes = ((mate, 0, 0, 2 * (1 - core)), ({"shot": 2 * first}, 1 + core, 1, 0), ({"shot": 2 * first + 1}, 1 + core, 1, 2))

    def c_copy(group, home):
        to, slot, at, h = homes[home]
        return pltpu.make_async_remote_copy(
            src_ref=part.at[group, at, :, pl.ds(h, 2)],
            dst_ref=final.at[strips(group), :, out_rows(band), :],
            send_sem=cs_sem.at[group, home], recv_sem=cr_sem.at[group, slot],
            device_id=to, device_id_type=MESH,
        )

    sources = (targets[0][2], band_a(chip_a), band_b(chip_b))

    def c_arrival(group, slot):
        ref = final.at[strips(group), :, out_rows(sources[slot]), :]
        return pltpu.make_async_copy(ref, ref, cr_sem.at[group, slot])

    def d_copy(group, i):
        ox, oy = to_whom(group, i)
        return pltpu.make_async_remote_copy(
            src_ref=final.at[group * SG + i], dst_ref=g_out.at[0, :, tile, 0],
            send_sem=d_sem.at[0], recv_sem=d_sem.at[1],
            device_id={"gx": ox, "gy": oy}, device_id_type=MESH,
        )

    def own_copy():
        return pltpu.make_async_copy(final.at[TILES - 1], g_out.at[0, :, tile, 0], d_sem.at[2])

    def from_second(group):
        b_copy(group).wait_recv()

        def body(i, carry):
            for at in (1, 0):
                part[group, at, i] = part[group, at, i] + half[group, at, i]
            return carry

        lax.fori_loop(0, SG, body, 0)
        for home in (1, 2, 0):
            c_copy(group, home).start()

        def keep(i, carry):
            final[group * SG + i, :, out_rows(band), :] = part[group, 0, i, pl.ds(2 * core, 2)]
            return carry

        lax.fori_loop(0, SG, keep, 0)

    def from_first(group):
        for slot in range(3):
            c_arrival(group, slot).wait()

        def body(i, carry):
            mine = (group == GROUPS - 1) & (i == SG - 1)

            @pl.when(mine)
            def _():
                own_copy().start()

            @pl.when(jnp.logical_not(mine))
            def _():
                d_copy(group, i).start()

            return carry

        lax.fori_loop(0, SG, body, 0)

    def stage(it, carry):
        @pl.when(it < GROUPS)
        def _():
            correlate(it)
            b_copy(it).start()

        @pl.when((it >= LAG_B) & (it < GROUPS + LAG_B))
        def _():
            from_second(it - LAG_B)

        @pl.when(it >= LAG_C)
        def _():
            from_first(it - LAG_C)

        return carry

    lax.fori_loop(0, GROUPS + LAG_C, stage, 0)

    for t in range(STEPS):
        for way in range(2):
            pl.when(x_to[way])(lambda: x_copy(t, way).wait_send())
            pl.when(y_to[way])(lambda: y_copy(t, way).wait_send())
            for f in range(2):
                pl.when(x_to[way])(lambda: z_copy(t + 1, way, f).wait_send())
        for target in range(3):
            for cut in range(3):
                e_copy(t + 1, target, cut).wait_send()
    for target in range(3):
        m_copy(target).wait_send()

    def drain(group, carry):
        b_copy(group).wait_send()
        for home in range(3):
            c_copy(group, home).wait_send()
        return carry

    lax.fori_loop(0, GROUPS, drain, 0)
    for copy in stores:
        copy.wait()
    own_copy().wait()
    sent = final.at[0 : TILES - 1]
    pltpu.make_async_copy(sent, sent, d_sem.at[0]).wait()
    arrived = g_out.at[0, :, 0 : TILES - 1, 0]
    pltpu.make_async_copy(arrived, arrived, d_sem.at[1]).wait()


def hand_over_kernel(a, b, c, x, y, z, sem):
    copies = []
    for v, w, dim in ((a, x, 1), (b, y, 1), (c, z, 2)):
        for i in range(4):
            piece = (slice(None),) * dim + (pl.ds(i * v.shape[dim] // 4, v.shape[dim] // 4),)
            copies.append(pltpu.make_async_copy(v.at[piece], w.at[piece], sem.at[len(copies)]))
    for copy in copies:
        copy.start()
    for copy in copies:
        copy.wait()


def body(vel_coef, src_prev, src_cur, rcv_prev, rcv_cur, src_pos, src_amp, rcv_pos, rcv_data, aperture, owner):
    big = [
        pltpu.with_memory_space_constraint(v, pltpu.HBM)
        for v in (
            vel_coef, src_prev, src_cur, rcv_prev, rcv_cur,
            rcv_pos, jnp.transpose(rcv_data, (1, 0, 2)), aperture, owner, src_amp,
        )
    ]
    whole = pl.BlockSpec(memory_space=pl.ANY)
    DMA = pltpu.SemaphoreType.DMA
    wave = pltpu.VMEM((2, CX + 2 * EDGE, CY + 16, NZ), F32)
    done = pl.pallas_call(
        main_kernel,
        out_shape=(
            jax.ShapeDtypeStruct(src_cur.shape, F32),
            jax.ShapeDtypeStruct(rcv_cur.shape, F32),
            jax.ShapeDtypeStruct((1, 2, TILES, 1, CY, NZ), F32),
        ),
        in_specs=[pl.BlockSpec(memory_space=pltpu.HBM)] * 10 + [pl.BlockSpec(memory_space=pltpu.SMEM)],
        out_specs=(whole, whole, whole),
        scratch_shapes=[
            wave, wave, wave, wave,
            pltpu.VMEM((STEPS, 4, 2, EXT, BAND, NZ), F32),
            pltpu.VMEM((2, CX, CY, NZ), F32),
            pltpu.VMEM((CX, CY, NZ), F32),
            pltpu.VMEM((STEPS, CX * CY, NZ), F32),
            pltpu.VMEM((STEPS, 2, 4 * CX, NZ), F32),
            pltpu.VMEM((STEPS, 2, 4 * CX, NZ), F32),
            pltpu.VMEM((GROUPS, CHIPS, SG, 4, BAND, NZ), F32),
            pltpu.VMEM((GROUPS, 2, SG, 4, BAND, NZ), F32),
            pltpu.VMEM((TILES, 2, CY, NZ), F32),
            pltpu.VMEM((4, 8, NZ), F32),
            pltpu.VMEM((TILES, NZ), jnp.int32),
            pltpu.SMEM((TILES, NZ), jnp.int32),
            pltpu.VMEM(rcv_pos.shape, jnp.int32),
            pltpu.VMEM((STEPS, 1, rcv_pos.shape[1]), F32),
            pltpu.VMEM(aperture.shape, jnp.int32),
            pltpu.VMEM(owner.shape, jnp.int32),
            pltpu.SMEM(src_amp.shape, F32),
            DMA((12,)),
            DMA((STEPS, 2)), DMA((STEPS, 2)), DMA((STEPS, 2)), DMA((STEPS, 2)),
            DMA((3,)), DMA((3,)),
            DMA((STEPS, 4, 3)), DMA((STEPS, 3, 3)),
            DMA((STEPS, 2, 2)), DMA((STEPS, 2, 2)),
            DMA((GROUPS,)), DMA((GROUPS,)),
            DMA((GROUPS, 3)), DMA((GROUPS, 3)),
            DMA((3,)), DMA((2,)),
        ],
        compiler_params=pltpu.CompilerParams(
            collective_id=0, has_side_effects=True, vmem_limit_bytes=48 * 1024 * 1024
        ),
        name="migrate",
    )(*big, src_pos)
    return pl.pallas_call(
        hand_over_kernel,
        out_shape=tuple(jax.ShapeDtypeStruct(v.shape, v.dtype) for v in done),
        in_specs=[whole] * 3,
        out_specs=(whole,) * 3,
        scratch_shapes=[DMA((12,))],
        compiler_params=pltpu.CompilerParams(vmem_limit_bytes=1024 * 1024),
        name="hand_over",
    )(*done)


def solution(mesh):
    return jax.shard_map(
        body,
        mesh=mesh,
        in_specs=(
            P("gx", "gy", None),
            P("shot", "gx", "gy", None),
            P("shot", "gx", "gy", None),
            P("shot", "gx", "gy", None),
            P("shot", "gx", "gy", None),
            P("shot"),
            P("shot", None),
            P("shot", None),
            P("shot", None, None),
            P("shot", None),
            P(),
        ),
        out_specs=(
            P("shot", "gx", "gy", None),
            P("shot", "gx", "gy", None),
            P(("gx", "gy"), "shot", None, None, None, None),
        ),
        check_vma=False,
    )
```
